32 devices in a mesh: node: 4 (over y, core), cores: 8 (over z, x).
Axes of the slice: x: 2, y: 2, z: 4, core: 2. Of those that a mesh axis runs over, the one named last changes fastest.
Arguments:
- fitted: bfloat16 [16, 256, 256, 256], P(None, ('node', 'cores')), may hold values from -0.09375 to 0.09375
- fit_mask: int32 [16, 32], replicated, may hold values 0 or 1
- tasks: int32 [16, 2], replicated, may hold values from 0 to 15, as said below
- owner_map: int32 [16], replicated, may hold values from 0 to 15, each once
- partner: int32 [4], replicated, may hold values from 0 to 3, as said below
- amplitudes: float32 [16, 4, 256, 256], P('cores', None, 'node'), may hold values from -6 to 6
- pair_energy: float32 [4], replicated, may hold values from -1.2 to -0.6
- virt_energy: float32 [1024], replicated, may hold values from 0.1 to 1.2
Outputs:
- new_amplitudes: float32 [16, 4, 256, 256], P('cores', None, 'node')
The draws below stay inside these ranges and needn't reach their ends.
Inputs may be any that keep to these rules, and one draw needn't show every extreme that they name: `tasks`: each row names an output tile pair and an input tile pair, both numbered X * 4 + Y; no two rows are equal. `owner_map`: each tile pair appears once. partner[partner[p]] = p and partner[p] != p.
All inputs are finite; a program needn't handle non-finite values.
Results may differ from the reference program's by a relative error of at most 0.00057.
Values may be sent and summed in bfloat16 or wider, within the bound.
No kernel may reach another device: no remote copies, remote signals or barrier semaphores. Data moves between devices by JAX's collectives and lax.ppermute only.
A program may use at most 192 MiB of HBM per device.

```python
import jax
import jax.numpy as jnp
from jax import lax

NT = 4
TILE = 256
AUX_DEV = 8
PAIRS = 4
TASKS = 16
NTP = 16
VIRT = 1024
BLOCKS = 32
NAUX = 256


def draw_tasks(key, part):
    chosen = jax.random.permutation(key, NTP * NTP)[:TASKS].astype(jnp.int32)
    return jnp.stack([chosen // NTP, chosen % NTP], axis=1).astype(jnp.int32)


def draw_partner(key, part):
    ordering = jax.random.permutation(key, PAIRS).astype(jnp.int32)
    first_half = ordering[0::2]
    second_half = ordering[1::2]
    linked = jnp.zeros((PAIRS,), jnp.int32).at[first_half].set(second_half)
    return linked.at[second_half].set(first_half)


def plant(array, own_key, low, high):
    index_at = [jax.random.randint(jax.random.fold_in(own_key, axis), (), 0, length) for axis, length in enumerate(array.shape)]
    widest = array.shape.index(max(array.shape))
    next_to = index_at[:widest] + [(index_at[widest] + 1) % array.shape[widest]] + index_at[widest + 1:]
    return array.at[tuple(index_at)].set(low).at[tuple(next_to)].set(high)


def shard_levels(own_key, dims, cuts, smallest, top_value):
    factor_of = 1.0
    for position, blocks in cuts:
        heights = jax.random.uniform(jax.random.fold_in(jax.random.fold_in(own_key, 6), position), (blocks,), jnp.float32, smallest / len(cuts), top_value / len(cuts))
        factor_of = factor_of * jnp.repeat(jnp.exp(heights), dims[position] // blocks).reshape((-1,) + (1,) * (len(dims) - 1 - position))
    return factor_of


def scatter_about(own_key, dims, width, bound, split=(), kind=jnp.bfloat16):
    values = width * jax.random.normal(own_key, dims, jnp.float32)
    if split:
        values = values * shard_levels(own_key, dims, split, -0.22, 0.18)
    return jnp.clip(values, -bound, bound).astype(kind)


def setup_inputs(seed: int = 0) -> dict:
    streams_of = jax.random.split(jax.random.key(seed), 9)
    return {
        "fitted": scatter_about(streams_of[0], (NTP, NAUX, TILE, TILE), (TILE * 16) ** -0.5, 0.09375, ((1, 32),)),
        "fit_mask": plant((jax.random.randint(streams_of[1], (NTP, BLOCKS), 0, 4) < 3).astype(jnp.int32), jax.random.fold_in(streams_of[1], 1), 0, 1),
        "tasks": draw_tasks(jax.random.fold_in(streams_of[8], 71), 0),
        "owner_map": jax.random.permutation(streams_of[3], NTP).astype(jnp.int32),
        "partner": draw_partner(jax.random.fold_in(streams_of[8], 71), 0),
        "amplitudes": scatter_about(streams_of[5], (NTP, PAIRS, TILE, TILE), 1.0, 6.0, ((0, 8), (2, 4)), jnp.float32),
        "pair_energy": jnp.clip(jax.random.uniform(streams_of[6], (PAIRS,), jnp.float32, -1.2, -0.6), -1.2, -0.6),
        "virt_energy": jnp.clip(jax.random.uniform(streams_of[7], (VIRT,), jnp.float32, 0.1, 1.2), 0.1, 1.2),
    }


def reference(fitted, fit_mask, tasks, owner_map, partner, amplitudes, pair_energy, virt_energy):
    places = jnp.arange(NTP, dtype=jnp.int32)
    slot_of = jnp.sum(jnp.where(owner_map[None, :] == places[:, None], places[None, :], 0), axis=1).astype(jnp.int32)
    lowered = amplitudes.astype(jnp.bfloat16)
    empty = jnp.zeros((PAIRS, TILE, TILE), jnp.float32)
    zero_index = jnp.zeros((), jnp.int32)

    def task_step(running, task_row):
        out_tile = task_row[0].astype(jnp.int32)
        in_tile = task_row[1].astype(jnp.int32)
        left_index = ((out_tile // NT) * NT + in_tile // NT).astype(jnp.int32)
        right_index = ((out_tile % NT) * NT + in_tile % NT).astype(jnp.int32)
        amp_tile = lowered[slot_of[in_tile]].astype(jnp.float32)

        def block_step(block_index, inner):
            block_index = jnp.asarray(block_index).astype(jnp.int32)
            weight = fit_mask[left_index, block_index] * fit_mask[right_index, block_index]
            start = (block_index * AUX_DEV).astype(jnp.int32)

            def compute(unused):
                left_factor = lax.dynamic_slice(fitted, (left_index, start, zero_index, zero_index), (1, AUX_DEV, TILE, TILE))[0].astype(jnp.float32)
                right_factor = lax.dynamic_slice(fitted, (right_index, start, zero_index, zero_index), (1, AUX_DEV, TILE, TILE))[0].astype(jnp.float32)
                half_product = jnp.einsum("qac,pcd->qpad", left_factor, amp_tile, precision=lax.Precision.HIGHEST)
                half_product = lax.optimization_barrier(half_product.astype(jnp.bfloat16)).astype(jnp.float32)
                return jnp.einsum("qpad,qbd->pab", half_product, right_factor, precision=lax.Precision.HIGHEST)

            def nothing(unused):
                return empty

            return inner + lax.cond(weight > 0, compute, nothing, 0)

        term = lax.fori_loop(0, BLOCKS, block_step, empty)
        return running.at[out_tile].add(term), None

    ladder_sum, unused_rows = lax.scan(task_step, jnp.zeros((NTP, PAIRS, TILE, TILE), jnp.float32), tasks)
    grid = ladder_sum.reshape(NT, NT, PAIRS, TILE, TILE)
    flipped = jnp.transpose(grid, (1, 0, 2, 4, 3)).reshape(NTP, PAIRS, TILE, TILE)
    flipped = jnp.take(flipped, partner, axis=0 + 1)
    symmetric = 0.5 * (ladder_sum + flipped)
    slot_sym = jnp.take(symmetric, owner_map, axis=0)
    row_tiles = owner_map // NT
    col_tiles = owner_map % NT
    offsets = jnp.arange(TILE, dtype=jnp.int32)
    row_energy = jnp.take(virt_energy, row_tiles[:, None] * TILE + offsets[None, :])
    col_energy = jnp.take(virt_energy, col_tiles[:, None] * TILE + offsets[None, :])
    denominator = (pair_energy[None, :, None, None] - row_energy[:, None, :, None]) - col_energy[:, None, None, :]
    return amplitudes + slot_sym / denominator
```

```python
import functools
import math

import jax
import jax.numpy as jnp
from jax import lax
from jax.experimental import pallas as pl
from jax.experimental.pallas import tpu as pltpu
from jax.sharding import PartitionSpec as P

AXES = ("node", "cores")


def ladder_kernel(
    dims, mask_ref, tasks_ref, owner_ref, partner_ref, fitted_ref, amps_ref, keep_ref, send_ref,
    left_buf, right_buf, tile_buf, total, work, slot_of, rank_of, load_sems, store_sems,
):
    nodes, cores, slots_here, pairs, rows, tile, aux, slots, side = dims
    task_count = tasks_ref.shape[0]
    node_index = lax.axis_index("node")
    core_index = lax.axis_index("cores")
    block = node_index * cores + core_index

    def invert(s, carry):
        slot_of[owner_ref[s]] = s
        return carry

    lax.fori_loop(0, slots, invert, 0)

    def rank(p, count):
        is_rep = p < partner_ref[p]

        @pl.when(is_rep)
        def _():
            rank_of[p] = count
            rank_of[partner_ref[p]] = count

        return count + is_rep.astype(jnp.int32)

    lax.fori_loop(0, pairs, rank, jnp.int32(0))

    def indices(t):
        out_tile = tasks_ref[t, 0]
        in_tile = tasks_ref[t, 1]
        a, b = out_tile // side, out_tile % side
        c, d = in_tile // side, in_tile % side
        return a, b, a * side + c, b * side + d, in_tile

    def enlist(t, count):
        _, _, left, right, _ = indices(t)
        work[count] = t
        return count + mask_ref[left, block] * mask_ref[right, block]

    active = lax.fori_loop(0, task_count, enlist, jnp.int32(0))

    def loads(i, slot):
        _, _, left, right, in_tile = indices(work[i])
        place = slot_of[in_tile]
        owner = place // slots_here
        inside = place % slots_here
        copies = [pltpu.make_async_copy(fitted_ref.at[left], left_buf.at[slot], load_sems.at[slot, 0])]
        for q in range(aux):
            copies.append(
                pltpu.make_async_copy(
                    fitted_ref.at[right, q], right_buf.at[slot, pairs, :, pl.ds(q * tile, tile)], load_sems.at[slot, 1]
                )
            )
        for n in range(nodes):
            copies.append(
                pltpu.make_async_copy(
                    amps_ref.at[n * cores + owner, inside],
                    tile_buf.at[slot, :, pl.ds(n * rows, rows), :],
                    load_sems.at[slot, 2],
                )
            )
        return copies

    @pl.when(active > 0)
    def _():
        for copy in loads(0, 0):
            copy.start()

    @pl.loop(0, slots)
    def _(s):
        total[s] = jnp.zeros(total.shape[1:], jnp.float32)

    @pl.loop(0, active)
    def _(i):
        slot = i % 2

        @pl.when(i + 1 < active)
        def _():
            for copy in loads(i + 1, 1 - slot):
                copy.start()

        for copy in loads(i, slot):
            copy.wait()
        a, b, _, _, _ = indices(work[i])
        straight = slot_of[a * side + b]
        crossed = slot_of[b * side + a]
        left_all = left_buf[slot].reshape(aux * tile, tile)
        for p in range(pairs):
            half = jnp.dot(left_all, tile_buf[slot, p], preferred_element_type=jnp.float32).astype(jnp.bfloat16)
            for q in range(aux):
                right_buf[slot, p, :, q * tile:(q + 1) * tile] = half[q * tile:(q + 1) * tile]
        for p in range(pairs):
            is_rep = p < partner_ref[p]
            first = jnp.where(is_rep, p, pairs)
            second = jnp.where(is_rep, pairs, p)
            place = jnp.where(is_rep, straight, crossed)
            which = rank_of[p]
            total[place, which] += lax.dot_general(
                right_buf[slot, first], right_buf[slot, second], (((1,), (1,)), ((), ())),
                preferred_element_type=jnp.float32,
            )

    mine = node_index % 2
    stores = [
        pltpu.make_async_copy(total.at[:, mine], keep_ref, store_sems.at[0]),
        pltpu.make_async_copy(total.at[:, 1 - mine], send_ref, store_sems.at[1]),
    ]
    for copy in stores:
        copy.start()
    for copy in stores:
        copy.wait()


def ladder_terms(mask, tasks, owner_map, partner, fitted, gathered, nodes, cores):
    tile_pairs, aux, tile, _ = fitted.shape
    slots_here, pairs, rows = gathered.shape[1:4]
    side = math.isqrt(tile_pairs)
    dims = (nodes, cores, slots_here, pairs, rows, tile, aux, tile_pairs, side)
    smem = pl.BlockSpec(memory_space=pltpu.SMEM)
    hbm = pl.BlockSpec(memory_space=pl.ANY)
    part = jax.ShapeDtypeStruct((tile_pairs, tile, tile), jnp.float32)
    return pl.pallas_call(
        functools.partial(ladder_kernel, dims),
        out_shape=(part, part),
        in_specs=[smem, smem, smem, smem, hbm, hbm],
        out_specs=(hbm, hbm),
        scratch_shapes=[
            pltpu.VMEM((2, aux, tile, tile), jnp.bfloat16),
            pltpu.VMEM((2, pairs + 1, tile, aux * tile), jnp.bfloat16),
            pltpu.VMEM((2, pairs, tile, tile), jnp.bfloat16),
            pltpu.VMEM((tile_pairs, pairs // 2, tile, tile), jnp.float32),
            pltpu.SMEM((tasks.shape[0] + 1,), jnp.int32),
            pltpu.SMEM((tile_pairs,), jnp.int32),
            pltpu.SMEM((pairs,), jnp.int32),
            pltpu.SemaphoreType.DMA((2, 3)),
            pltpu.SemaphoreType.DMA((2,)),
        ],
        compiler_params=pltpu.CompilerParams(vmem_limit_bytes=48 * 1024 * 1024),
        cost_estimate=pl.CostEstimate(flops=40 * 10**9, bytes_accessed=48 * 2**20, transcendentals=0),
        name="ladder",
    )(mask, tasks, owner_map, partner, fitted, gathered)


def swap(array, mask, total):
    return lax.ppermute(array, AXES, [(i, i ^ mask) for i in range(total)])


def pick(array, index, axis):
    return lax.dynamic_index_in_dim(array, index, axis, keepdims=False)


def body(nodes, cores, fitted, fit_mask, tasks, owner_map, partner, amplitudes, pair_energy, virt_energy):
    slots_here, pairs, rows, tile = amplitudes.shape
    tile_pairs = owner_map.shape[0]
    side = math.isqrt(tile_pairs)
    total = nodes * cores
    node_index = lax.axis_index("node")
    core_index = lax.axis_index("cores")
    f32, f16 = jnp.float32, jnp.float16
    scale = 2.0 ** -9

    lowered = amplitudes.astype(jnp.bfloat16)
    gathered = lax.all_gather(lowered, AXES, axis=0, tiled=False)
    keep, send = ladder_terms(fit_mask, tasks, owner_map, partner, fitted, gathered, nodes, cores)

    got = swap(send, cores, total)
    inner = nodes // 2
    cuts = inner // slots_here
    strip = rows // cuts
    part = (keep + got) * scale
    part = part.reshape(cores, slots_here, nodes, cuts, strip, tile).transpose(0, 1, 3, 2, 4, 5)
    part = part.reshape(cores, inner, nodes * strip, tile).astype(f16)

    def halve(value, index, axis_size, axis, mask):
        shape = value.shape
        inner_shape = (axis_size // 2, 2)
        split = value.reshape(shape[:axis] + inner_shape + shape[axis + 1:])
        other = swap(pick(split, 1 - index, axis + 1), mask, total)
        own = pick(split, index, axis + 1)
        return (own.astype(f32) + other.astype(f32)).astype(f16)

    def over_inner(value):
        mask, index = 2 * cores, node_index // 2
        while value.shape[1] > 1:
            value = halve(value, index % 2, value.shape[1], 1, mask)
            mask, index = mask * 2, index // 2
        return value[:, 0]

    def over_low(value):
        return halve(value, core_index % 2, value.shape[0], 0, 1)

    half_rows = part.shape[2] // 2
    upper = over_low(over_inner(part[:, :, :half_rows]))
    lower = over_inner(over_low(part[:, :, half_rows:]))
    part = jnp.concatenate([upper, lower], axis=1)
    far = part.shape[0]
    at = core_index // 2
    mine = pick(part, at, 0).astype(f32)
    for step in range(1, far):
        mine = mine + swap(pick(part, at ^ step, 0), 2 * step, total).astype(f32)

    mine = mine * (0.5 / scale)
    blocks_here = slots_here * 2
    straight = mine.reshape(nodes, strip, tile)
    turned = mine.reshape(nodes, strip, nodes, rows).transpose(2, 3, 0, 1)
    if cuts == 1:
        both = jnp.stack([straight, turned.reshape(nodes, rows, tile)], axis=1)
        every = lax.all_to_all(both, "node", 0, 0, tiled=True)
        own_rows = every[:, 0]
        own_cols = every[:, 1]
    else:
        own_rows = lax.all_to_all(straight, "node", 0, 0, tiled=True)
        own_rows = own_rows.reshape(slots_here, cuts, 2, strip, tile).transpose(0, 2, 1, 3, 4)
        own_cols = lax.all_to_all(turned, "node", 0, 0, tiled=True)
        own_cols = own_cols.reshape(slots_here, cuts, 2, rows, nodes, strip).transpose(0, 2, 3, 4, 1, 5)
    own_rows = own_rows.reshape(slots_here, 2, rows, tile)
    own_cols = own_cols.reshape(slots_here, 2, rows, tile)
    all_cols = lax.all_gather(own_cols, "cores", axis=0, tiled=True)

    places = jnp.arange(tile_pairs, dtype=jnp.int32)
    slot_of = jnp.sum(jnp.where(owner_map[None, :] == places[:, None], places[None, :], 0), axis=1)
    my_tiles = lax.dynamic_slice_in_dim(owner_map, core_index * slots_here, slots_here)
    row_tiles, col_tiles = my_tiles // side, my_tiles % side
    pair_ids = jnp.arange(pairs, dtype=jnp.int32)
    is_rep = pair_ids < partner
    low = jnp.minimum(pair_ids, partner)
    ranks = jnp.sum((is_rep[None, :] & (pair_ids[None, :] < low[:, None])).astype(jnp.int32), axis=1)
    out = []
    for j in range(slots_here):
        crossed = pick(all_cols, slot_of[col_tiles[j] * side + row_tiles[j]], 0)
        symmetric = jnp.stack(
            [jnp.where(is_rep[p], pick(own_rows[j], ranks[p], 0), pick(crossed, ranks[p], 0)) for p in range(pairs)]
        )
        row_energy = lax.dynamic_slice_in_dim(virt_energy, row_tiles[j] * tile + node_index * rows, rows)
        col_energy = lax.dynamic_slice_in_dim(virt_energy, col_tiles[j] * tile, tile)
        denominator = (pair_energy[:, None, None] - row_energy[None, :, None]) - col_energy[None, None, :]
        out.append(amplitudes[j] + symmetric / denominator)
    return jnp.stack(out)


def solution(mesh):
    placed = (P(None, AXES, None, None), P(), P(), P(), P(), P("cores", None, "node", None), P(), P())
    return jax.shard_map(
        functools.partial(body, mesh.shape["node"], mesh.shape["cores"]),
        mesh=mesh, in_specs=placed, out_specs=P("cores", None, "node", None), check_vma=False,
    )
```

```python
import functools
import math

import jax
import jax.numpy as jnp
from jax import lax
from jax.experimental import pallas as pl
from jax.experimental.pallas import tpu as pltpu
from jax.sharding import PartitionSpec as P

AXES = ("node", "cores")


def ladder_kernel(
    dims, mask_ref, tasks_ref, owner_ref, fitted_ref, amps_ref, keep_ref, send_ref,
    left_buf, right_buf, half_buf, tile_buf, total, work, slot_of, load_sems, store_sems,
):
    nodes, cores, slots_here, rows, tile, aux, slots, side = dims
    task_count = tasks_ref.shape[0]
    node_index = lax.axis_index("node")
    core_index = lax.axis_index("cores")
    block = node_index * cores + core_index

    def invert(s, carry):
        slot_of[owner_ref[s]] = s
        return carry

    lax.fori_loop(0, slots, invert, 0)

    def indices(t):
        out_tile = tasks_ref[t, 0]
        in_tile = tasks_ref[t, 1]
        a, b = out_tile // side, out_tile % side
        c, d = in_tile // side, in_tile % side
        return a, b, a * side + c, b * side + d, in_tile

    def enlist(t, count):
        _, _, left, right, _ = indices(t)
        work[count] = t
        return count + mask_ref[left, block] * mask_ref[right, block]

    active = lax.fori_loop(0, task_count, enlist, jnp.int32(0))

    def loads(i, slot):
        _, _, left, right, in_tile = indices(work[i])
        place = slot_of[in_tile]
        owner = place // slots_here
        inside = place % slots_here
        copies = [pltpu.make_async_copy(fitted_ref.at[left], left_buf.at[slot], load_sems.at[slot, 0])]
        for q in range(aux):
            copies.append(
                pltpu.make_async_copy(
                    fitted_ref.at[right, q], right_buf.at[slot, :, pl.ds(q * tile, tile)], load_sems.at[slot, 1]
                )
            )
        for n in range(nodes):
            copies.append(
                pltpu.make_async_copy(
                    amps_ref.at[n * cores + owner, inside],
                    tile_buf.at[slot, :, pl.ds(n * rows, rows), :],
                    load_sems.at[slot, 2],
                )
            )
        return copies

    @pl.when(active > 0)
    def _():
        for copy in loads(0, 0):
            copy.start()

    @pl.loop(0, slots)
    def _(s):
        total[s] = jnp.zeros(total.shape[1:], jnp.float32)

    def contract(first, second):
        return lax.dot_general(first, second, (((1,), (1,)), ((), ())), preferred_element_type=jnp.float32)

    @pl.loop(0, active)
    def _(i):
        slot = i % 2

        @pl.when(i + 1 < active)
        def _():
            for copy in loads(i + 1, 1 - slot):
                copy.start()

        for copy in loads(i, slot):
            copy.wait()
        a, b, _, _, _ = indices(work[i])
        straight = slot_of[a * side + b]
        crossed = slot_of[b * side + a]
        left_all = left_buf[slot].reshape(aux * tile, tile)
        for p in range(2):
            half = jnp.dot(left_all, tile_buf[slot, p], preferred_element_type=jnp.float32).astype(jnp.bfloat16)
            for q in range(aux):
                half_buf[p, :, q * tile:(q + 1) * tile] = half[q * tile:(q + 1) * tile]
        shape = total.shape[1:]
        total[straight] += contract(half_buf[0], right_buf[slot]).reshape(shape)
        total[crossed] += contract(right_buf[slot], half_buf[1]).reshape(shape)

    mine = node_index % 2
    stores = [
        pltpu.make_async_copy(total.at[:, :, mine], keep_ref, store_sems.at[0]),
        pltpu.make_async_copy(total.at[:, :, 1 - mine], send_ref, store_sems.at[1]),
    ]
    for copy in stores:
        copy.start()
    for copy in stores:
        copy.wait()


def ladder_terms(mask, tasks, owner_map, fitted, gathered, nodes, cores):
    tile_pairs, aux, tile, _ = fitted.shape
    slots_here, _, rows = gathered.shape[1:4]
    side = math.isqrt(tile_pairs)
    dims = (nodes, cores, slots_here, rows, tile, aux, tile_pairs, side)
    smem = pl.BlockSpec(memory_space=pltpu.SMEM)
    hbm = pl.BlockSpec(memory_space=pl.ANY)
    part = jax.ShapeDtypeStruct((tile_pairs, nodes // 2, rows, tile), jnp.float32)
    return pl.pallas_call(
        functools.partial(ladder_kernel, dims),
        out_shape=(part, part),
        in_specs=[smem, smem, smem, hbm, hbm],
        out_specs=(hbm, hbm),
        scratch_shapes=[
            pltpu.VMEM((2, aux, tile, tile), jnp.bfloat16),
            pltpu.VMEM((2, tile, aux * tile), jnp.bfloat16),
            pltpu.VMEM((2, tile, aux * tile), jnp.bfloat16),
            pltpu.VMEM((2, 2, tile, tile), jnp.bfloat16),
            pltpu.VMEM((tile_pairs, nodes // 2, 2, rows, tile), jnp.float32),
            pltpu.SMEM((tasks.shape[0] + 1,), jnp.int32),
            pltpu.SMEM((tile_pairs,), jnp.int32),
            pltpu.SemaphoreType.DMA((2, 3)),
            pltpu.SemaphoreType.DMA((2,)),
        ],
        compiler_params=pltpu.CompilerParams(vmem_limit_bytes=32 * 1024 * 1024),
        cost_estimate=pl.CostEstimate(flops=20 * 10**9, bytes_accessed=30 * 2**20, transcendentals=0),
        name="ladder",
    )(mask, tasks, owner_map, fitted, gathered)


def swap(array, mask, total):
    return lax.ppermute(array, AXES, [(i, i ^ mask) for i in range(total)])


def pick(array, index, axis):
    return lax.dynamic_index_in_dim(array, index, axis, keepdims=False)


def halve(value, index, axis, mask, total):
    shape = value.shape
    split = value.reshape(shape[:axis] + (shape[axis] // 2, 2) + shape[axis + 1:])
    other = swap(pick(split, 1 - index, axis + 1), mask, total)
    own = pick(split, index, axis + 1)
    return (own.astype(jnp.float32) + other.astype(jnp.float32)).astype(value.dtype)


def reduce_blocks(keep, send, nodes, cores, scale):
    total = nodes * cores
    node_index = lax.axis_index("node")
    core_index = lax.axis_index("cores")
    slots, inner, rows, tile = keep.shape
    got = swap(send, cores, total)
    part = ((keep + got) * scale).astype(jnp.float16).reshape(cores, slots // cores, inner, rows, tile)

    def over_inner(value):
        mask, index = 2 * cores, node_index // 2
        while value.shape[2] > 1:
            value = halve(value, index % 2, 2, mask, total)
            mask, index = mask * 2, index // 2
        return value

    def over_low(value):
        return halve(value, core_index % 2, 0, 1, total)

    upper = over_low(over_inner(part[:, :, :, :rows // 2]))
    lower = over_inner(over_low(part[:, :, :, rows // 2:]))
    part = jnp.concatenate([upper, lower], axis=3)[:, :, 0]
    at = core_index // 2
    mine = pick(part, at, 0).astype(jnp.float32)
    for step in range(1, part.shape[0]):
        mine = mine + swap(pick(part, at ^ step, 0), 2 * step, total).astype(jnp.float32)
    return mine * (0.5 / scale)


def turn_blocks(mine, nodes, cores, scale):
    total = nodes * cores
    slots_here, rows, tile = mine.shape
    node_index = lax.axis_index("node")
    turned = (mine * scale).astype(jnp.float16).reshape(slots_here * rows, tile).T
    turned = turned.reshape(nodes, rows, slots_here * rows)
    pieces = [swap(pick(turned, node_index ^ step, 0), step * cores, total) for step in range(1, nodes)]
    pieces = jnp.stack([pick(turned, node_index, 0)] + pieces)
    every = lax.all_gather(pieces, "cores", axis=0, tiled=False)
    return every


def strips(every, place, node_index, slots_here, scale):
    _, nodes, rows, width = every.shape
    owner, inside = place // slots_here, place % slots_here
    block = pick(every, owner, 0).reshape(nodes, rows, slots_here, width // slots_here)
    block = pick(block, inside, 2).astype(jnp.float32) * (1.0 / scale)
    ordered = [pick(block, node_index ^ n, 0) for n in range(nodes)]
    return jnp.concatenate(ordered, axis=1)


def body(nodes, cores, fitted, fit_mask, tasks, owner_map, partner, amplitudes, pair_energy, virt_energy):
    slots_here, pairs, rows, tile = amplitudes.shape
    tile_pairs = owner_map.shape[0]
    side = math.isqrt(tile_pairs)
    node_index = lax.axis_index("node")
    core_index = lax.axis_index("cores")
    scale = 2.0 ** -9

    pair_ids = jnp.arange(pairs, dtype=jnp.int32)
    is_rep = pair_ids < partner
    low = jnp.minimum(pair_ids, partner)
    ranks = jnp.sum((is_rep[None, :] & (pair_ids[None, :] < low[:, None])).astype(jnp.int32), axis=1)
    groups = pairs // 2
    pair_of = [jnp.sum(jnp.where(is_rep & (ranks == g), pair_ids, 0)) for g in range(groups)]
    twin_of = [jnp.sum(jnp.where(~is_rep & (ranks == g), pair_ids, 0)) for g in range(groups)]
    places = jnp.arange(tile_pairs, dtype=jnp.int32)
    slot_of = jnp.sum(jnp.where(owner_map[None, :] == places[:, None], places[None, :], 0), axis=1)
    my_tiles = lax.dynamic_slice_in_dim(owner_map, core_index * slots_here, slots_here)
    row_tiles, col_tiles = my_tiles // side, my_tiles % side

    gathered = []
    for g in range(groups):
        chosen = jnp.stack([pick(amplitudes, pair_of[g], 1), pick(amplitudes, twin_of[g], 1)], axis=1)
        lowered = chosen.astype(jnp.bfloat16)
        if gathered:
            lowered, gathered[-1] = lax.optimization_barrier((lowered, gathered[-1]))
        gathered.append(lax.all_gather(lowered, AXES, axis=0, tiled=False))
    straight, crossed = [], []
    for g in range(groups):
        keep, send = ladder_terms(fit_mask, tasks, owner_map, fitted, gathered[g], nodes, cores)
        mine = reduce_blocks(keep, send, nodes, cores, scale)
        straight.append(mine)
        crossed.append(turn_blocks(mine, nodes, cores, scale))
    out = []
    for j in range(slots_here):
        place = slot_of[col_tiles[j] * side + row_tiles[j]]
        turned = [strips(crossed[g], place, node_index, slots_here, scale) for g in range(groups)]
        symmetric = []
        for p in range(pairs):
            same = straight[0][j]
            other = turned[0]
            for g in range(1, groups):
                same = jnp.where(ranks[p] == g, straight[g][j], same)
                other = jnp.where(ranks[p] == g, turned[g], other)
            symmetric.append(jnp.where(is_rep[p], same, other))
        row_energy = lax.dynamic_slice_in_dim(virt_energy, row_tiles[j] * tile + node_index * rows, rows)
        col_energy = lax.dynamic_slice_in_dim(virt_energy, col_tiles[j] * tile, tile)
        denominator = (pair_energy[:, None, None] - row_energy[None, :, None]) - col_energy[None, None, :]
        out.append(amplitudes[j] + jnp.stack(symmetric) / denominator)
    return jnp.stack(out)


def solution(mesh):
    placed = (P(None, AXES, None, None), P(), P(), P(), P(), P("cores", None, "node", None), P(), P())
    return jax.shard_map(
        functools.partial(body, mesh.shape["node"], mesh.shape["cores"]),
        mesh=mesh, in_specs=placed, out_specs=P("cores", None, "node", None), check_vma=False,
    )
```

```python
import functools
import math

import jax
import jax.numpy as jnp
from jax import lax
from jax.experimental import pallas as pl
from jax.experimental.pallas import tpu as pltpu
from jax.sharding import PartitionSpec as P

AXES = ("node", "cores")


def ladder_kernel(dims, mask_ref, tasks_ref, owner_ref, fitted_ref, *refs):
    nodes, cores, slots_here, rows, tile, aux, slots, side = dims
    first_refs, second_refs, refs = refs[:nodes], refs[nodes:nodes + 4], refs[nodes + 4:]
    keep_ref, send_ref, left_buf, right_buf, half_buf, tile_buf, total, work, slot_of, load_sems, store_sems = refs
    task_count = tasks_ref.shape[0]
    node_index = lax.axis_index("node")
    core_index = lax.axis_index("cores")
    block = node_index * cores + core_index

    def invert(s, carry):
        slot_of[owner_ref[s]] = s
        return carry

    lax.fori_loop(0, slots, invert, 0)

    def indices(t):
        out_tile = tasks_ref[t, 0]
        in_tile = tasks_ref[t, 1]
        a, b = out_tile // side, out_tile % side
        c, d = in_tile // side, in_tile % side
        return a, b, a * side + c, b * side + d, in_tile

    def enlist(t, count):
        _, _, left, right, _ = indices(t)
        work[count] = t
        return count + mask_ref[left, block] * mask_ref[right, block]

    active = lax.fori_loop(0, task_count, enlist, jnp.int32(0))

    def start_loads(i, slot):
        _, _, left, right, in_tile = indices(work[i])
        place = slot_of[in_tile]
        inside = place % slots_here
        apart = (place // slots_here) ^ core_index
        low, far = apart % 2, apart // 2

        def fetch(source, p, other):
            strip = pl.ds(pl.multiple_of((node_index ^ other) * rows, rows), rows)
            pltpu.make_async_copy(source, tile_buf.at[slot, p, strip, :], load_sems.at[slot, 2]).start()

        for other in range(nodes):
            fetch(first_refs[other].at[low, far, inside], 0, other)
        for x in range(2):

            @pl.when(low == x)
            def _():
                for other in range(nodes):
                    fetch(second_refs[(other % 2) * 2 + x].at[other // 2, far, inside], 1, other)

        pltpu.make_async_copy(fitted_ref.at[left], left_buf.at[slot], load_sems.at[slot, 0]).start()
        for q in range(aux):
            pltpu.make_async_copy(
                fitted_ref.at[right, q], right_buf.at[slot, :, pl.ds(q * tile, tile)], load_sems.at[slot, 1]
            ).start()

    def wait_loads(slot):
        for k, buf in enumerate((left_buf, right_buf, tile_buf)):
            pltpu.make_async_copy(buf.at[slot], buf.at[slot], load_sems.at[slot, k]).wait()

    @pl.when(active > 0)
    def _():
        start_loads(0, 0)

    @pl.loop(0, slots)
    def _(s):
        total[s] = jnp.zeros(total.shape[1:], jnp.float32)

    def contract(first, second):
        return lax.dot_general(first, second, (((1,), (1,)), ((), ())), preferred_element_type=jnp.float32)

    @pl.loop(0, active)
    def _(i):
        slot = i % 2

        @pl.when(i + 1 < active)
        def _():
            start_loads(i + 1, 1 - slot)

        wait_loads(slot)
        a, b, _, _, _ = indices(work[i])
        straight = slot_of[a * side + b]
        crossed = slot_of[b * side + a]
        left_all = left_buf[slot].reshape(aux * tile, tile)
        for p in range(2):
            half = jnp.dot(left_all, tile_buf[slot, p], preferred_element_type=jnp.float32).astype(jnp.bfloat16)
            for q in range(aux):
                half_buf[p, :, q * tile:(q + 1) * tile] = half[q * tile:(q + 1) * tile]
        shape = total.shape[1:]
        total[straight] += contract(half_buf[0], right_buf[slot]).reshape(shape)
        total[crossed] += contract(right_buf[slot], half_buf[1]).reshape(shape)

    mine = node_index % 2
    stores = [
        pltpu.make_async_copy(total.at[:, :, mine], keep_ref, store_sems.at[0]),
        pltpu.make_async_copy(total.at[:, :, 1 - mine], send_ref, store_sems.at[1]),
    ]
    for copy in stores:
        copy.start()
    for copy in stores:
        copy.wait()


def ladder_terms(mask, tasks, owner_map, fitted, first, second, nodes, cores):
    tile_pairs, aux, tile, _ = fitted.shape
    slots_here, rows = first[0].shape[2:4]
    side = math.isqrt(tile_pairs)
    dims = (nodes, cores, slots_here, rows, tile, aux, tile_pairs, side)
    smem = pl.BlockSpec(memory_space=pltpu.SMEM)
    hbm = pl.BlockSpec(memory_space=pl.ANY)
    part = jax.ShapeDtypeStruct((tile_pairs, nodes // 2, rows, tile), jnp.float32)
    return pl.pallas_call(
        functools.partial(ladder_kernel, dims),
        out_shape=(part, part),
        in_specs=[smem, smem, smem] + [hbm] * (1 + len(first) + len(second)),
        out_specs=(hbm, hbm),
        scratch_shapes=[
            pltpu.VMEM((2, aux, tile, tile), jnp.bfloat16),
            pltpu.VMEM((2, tile, aux * tile), jnp.bfloat16),
            pltpu.VMEM((2, tile, aux * tile), jnp.bfloat16),
            pltpu.VMEM((2, 2, tile, tile), jnp.bfloat16),
            pltpu.VMEM((tile_pairs, nodes // 2, 2, rows, tile), jnp.float32),
            pltpu.SMEM((tasks.shape[0] + 1,), jnp.int32),
            pltpu.SMEM((tile_pairs,), jnp.int32),
            pltpu.SemaphoreType.DMA((2, 3)),
            pltpu.SemaphoreType.DMA((2,)),
        ],
        compiler_params=pltpu.CompilerParams(vmem_limit_bytes=32 * 1024 * 1024),
        cost_estimate=pl.CostEstimate(flops=20 * 10**9, bytes_accessed=30 * 2**20, transcendentals=0),
        name="ladder",
    )(mask, tasks, owner_map, fitted, *first, *second)


def swap(array, mask, total):
    return lax.ppermute(array, AXES, [(i, i ^ mask) for i in range(total)])


def pick(array, index, axis):
    return lax.dynamic_index_in_dim(array, index, axis, keepdims=False)


def halve(value, index, axis, mask, total):
    shape = value.shape
    split = value.reshape(shape[:axis] + (shape[axis] // 2, 2) + shape[axis + 1:])
    other = swap(pick(split, 1 - index, axis + 1), mask, total)
    own = pick(split, index, axis + 1)
    return (own.astype(jnp.float32) + other.astype(jnp.float32)).astype(value.dtype)


def reduce_blocks(keep, send, nodes, cores, scale):
    total = nodes * cores
    node_index = lax.axis_index("node")
    core_index = lax.axis_index("cores")
    slots, inner, rows, tile = keep.shape
    got = swap(send, cores, total)
    part = ((keep + got) * scale).astype(jnp.float16).reshape(cores, slots // cores, inner, rows, tile)

    def over_inner(value):
        mask, index = 2 * cores, node_index // 2
        while value.shape[2] > 1:
            value = halve(value, index % 2, 2, mask, total)
            mask, index = mask * 2, index // 2
        return value

    def over_low(value):
        return halve(value, core_index % 2, 0, 1, total)

    upper = over_low(over_inner(part[:, :, :, :rows // 2]))
    lower = over_inner(over_low(part[:, :, :, rows // 2:]))
    part = jnp.concatenate([upper, lower], axis=3)[:, :, 0]
    at = core_index // 2
    mine = pick(part, at, 0).astype(jnp.float32)
    for step in range(1, part.shape[0]):
        mine = mine + swap(pick(part, at ^ step, 0), 2 * step, total).astype(jnp.float32)
    return mine * (0.5 / scale)


def pair_groups(partner_ref, pairs):
    count = jnp.int32(0)
    chosen = [jnp.int32(0)] * (pairs // 2)
    for p in range(pairs):
        is_rep = p < partner_ref[p]
        chosen = [jnp.where(is_rep & (count == g), p, old) for g, old in enumerate(chosen)]
        count = count + is_rep.astype(jnp.int32)
    return [(p, partner_ref[p]) for p in chosen]


def lower_kernel(partner_ref, amps_ref, *out_refs):
    for g, both in enumerate(pair_groups(partner_ref, amps_ref.shape[1])):
        for role, p in enumerate(both):
            out_refs[2 * g + role][...] = amps_ref[:, p].astype(jnp.bfloat16)


def lower(partner, amplitudes):
    slots_here, pairs, rows, tile = amplitudes.shape
    vmem = pl.BlockSpec(memory_space=pltpu.VMEM)
    return pl.pallas_call(
        lower_kernel,
        out_shape=(jax.ShapeDtypeStruct((slots_here, rows, tile), jnp.bfloat16),) * pairs,
        in_specs=[pl.BlockSpec(memory_space=pltpu.SMEM), vmem],
        out_specs=(vmem,) * pairs,
        name="lower",
    )(partner, amplitudes)


def spread_far(part, cores, total):
    return jnp.stack([part] + [swap(part, 2 * step, total) for step in range(1, cores // 2)])


def spread_first(part, nodes, cores):
    total = nodes * cores
    part = spread_far(part, cores, total)
    pieces = {0: jnp.stack([part, swap(part, 1, total)])}
    bit = nodes // 2
    while bit:
        pieces.update({other | bit: swap(piece, bit * cores, total) for other, piece in pieces.items()})
        bit //= 2
    return [pieces[other] for other in range(nodes)]


def spread_second(part, nodes, cores):
    total = nodes * cores
    pieces = {0: spread_far(part, cores, total)}
    bit = nodes // 2
    while bit > 1:
        pieces.update({other | bit: swap(piece, bit * cores, total) for other, piece in pieces.items()})
        bit //= 2
    near = jnp.stack([pieces[2 * upper] for upper in range(nodes // 2)])
    far = swap(near, 1, total)
    return [near, far, swap(near, cores, total), swap(far, cores, total)]


def turn_blocks(mine, far_first, nodes, cores, scale):
    total = nodes * cores
    slots_here, rows, tile = mine.shape
    node_index = lax.axis_index("node")
    turned = (mine * scale).astype(jnp.float16).reshape(slots_here * rows, tile).T
    turned = turned.reshape(nodes, rows, slots_here * rows)
    pieces = [pick(turned, node_index, 0)]
    pieces += [swap(pick(turned, node_index ^ step, 0), step * cores, total) for step in range(1, nodes)]
    pieces = jnp.stack(pieces)
    block = jnp.stack([pick(pieces, node_index ^ n, 0) for n in range(nodes)])
    block = block.reshape(nodes, rows, slots_here, rows).transpose(2, 1, 0, 3).reshape(slots_here, rows, tile)
    if far_first:
        near = spread_far(block, cores, total)
        every = jnp.stack([near, swap(near, 1, total)], axis=1)
    else:
        every = spread_far(jnp.stack([block, swap(block, 1, total)]), cores, total)
    return every.reshape(cores, slots_here, rows, tile).astype(jnp.float32) * (1.0 / scale)


def update_kernel(side, owner_ref, partner_ref, pair_ref, energy_ref, column_ref, amps_ref, *refs):
    slots_here, pairs, rows, tile = amps_ref.shape
    groups = pairs // 2
    straight, crossed, out_ref, slot_of = refs[:groups], refs[groups:2 * groups], refs[-2], refs[-1]
    node_index = lax.axis_index("node")
    core_index = lax.axis_index("cores")

    def invert(s, carry):
        slot_of[owner_ref[s]] = s
        return carry

    lax.fori_loop(0, owner_ref.shape[0], invert, 0)
    for j in range(slots_here):
        mine = owner_ref[core_index * slots_here + j]
        row_tile, col_tile = mine // side, mine % side
        place = slot_of[col_tile * side + row_tile]
        apart, inside = (place // slots_here) ^ core_index, place % slots_here
        row_energy = energy_ref[pl.ds(pl.multiple_of(row_tile * tile + node_index * rows, 8), rows), :]
        col_energy = column_ref[pl.ds(col_tile, 1), :]
        for g, (rep, twin) in enumerate(pair_groups(partner_ref, pairs)):
            for p, value in ((rep, straight[g][j]), (twin, crossed[g][apart, inside])):
                denominator = (pair_ref[p] - row_energy) - col_energy
                out_ref[j, p] = amps_ref[j, p] + value / denominator


def update(owner_map, partner, pair_energy, virt_energy, amplitudes, straight, crossed):
    tile = amplitudes.shape[3]
    smem = pl.BlockSpec(memory_space=pltpu.SMEM)
    vmem = pl.BlockSpec(memory_space=pltpu.VMEM)
    return pl.pallas_call(
        functools.partial(update_kernel, math.isqrt(owner_map.shape[0])),
        out_shape=jax.ShapeDtypeStruct(amplitudes.shape, jnp.float32),
        in_specs=[smem] * 3 + [vmem] * (3 + len(straight) + len(crossed)),
        out_specs=vmem,
        scratch_shapes=[pltpu.SMEM(owner_map.shape, jnp.int32)],
        compiler_params=pltpu.CompilerParams(vmem_limit_bytes=32 * 1024 * 1024),
        name="update",
    )(
        owner_map, partner, pair_energy, virt_energy.reshape(-1, 1), virt_energy.reshape(-1, tile),
        amplitudes, *straight, *crossed,
    )


def body(nodes, cores, fitted, fit_mask, tasks, owner_map, partner, amplitudes, pair_energy, virt_energy):
    scale = 2.0 ** -9
    parts = lower(partner, amplitudes)
    groups = len(parts) // 2
    first = [spread_first(parts[2 * g], nodes, cores) for g in range(groups)]
    second = [spread_second(parts[2 * g + 1], nodes, cores) for g in range(groups)]
    straight, crossed = [], []
    for g in range(groups):
        keep, send = ladder_terms(fit_mask, tasks, owner_map, fitted, first[g], second[g], nodes, cores)
        mine = reduce_blocks(keep, send, nodes, cores, scale)
        straight.append(mine)
        crossed.append(turn_blocks(mine, g == 0, nodes, cores, scale))
    return update(owner_map, partner, pair_energy, virt_energy, amplitudes, straight, crossed)


def solution(mesh):
    placed = (P(None, AXES, None, None), P(), P(), P(), P(), P("cores", None, "node", None), P(), P())
    return jax.shard_map(
        functools.partial(body, mesh.shape["node"], mesh.shape["cores"]),
        mesh=mesh, in_specs=placed, out_specs=P("cores", None, "node", None), check_vma=False,
    )
```

```python
import functools
import math

import jax
import jax.numpy as jnp
from jax import lax
from jax.experimental import pallas as pl
from jax.experimental.pallas import tpu as pltpu
from jax.sharding import PartitionSpec as P

AXES = ("node", "cores")


def ladder_kernel(dims, mask_ref, tasks_ref, owner_ref, fitted_ref, *refs):
    nodes, cores, slots_here, rows, tile, aux, slots, side = dims
    first_refs, second_refs, refs = refs[:nodes], refs[nodes:nodes + 4], refs[nodes + 4:]
    keep_ref, send_ref, left_buf, right_buf, half_buf, tile_buf, total, work, slot_of, load_sems, store_sems = refs
    task_count = tasks_ref.shape[0]
    node_index = lax.axis_index("node")
    core_index = lax.axis_index("cores")
    block = node_index * cores + core_index

    def invert(s, carry):
        slot_of[owner_ref[s]] = s
        return carry

    lax.fori_loop(0, slots, invert, 0)

    def indices(t):
        out_tile = tasks_ref[t, 0]
        in_tile = tasks_ref[t, 1]
        a, b = out_tile // side, out_tile % side
        c, d = in_tile // side, in_tile % side
        return a, b, a * side + c, b * side + d, in_tile

    def enlist(t, count):
        _, _, left, right, _ = indices(t)
        work[count] = t
        return count + mask_ref[left, block] * mask_ref[right, block]

    active = lax.fori_loop(0, task_count, enlist, jnp.int32(0))

    def start_loads(i, slot):
        _, _, left, right, in_tile = indices(work[i])
        place = slot_of[in_tile]
        inside = place % slots_here
        apart = (place // slots_here) ^ core_index
        low, far = apart % 2, apart // 2

        def fetch(source, p, other):
            strip = pl.ds(pl.multiple_of((node_index ^ other) * rows, rows), rows)
            pltpu.make_async_copy(source, tile_buf.at[slot, p, strip, :], load_sems.at[slot, 2]).start()

        for other in range(nodes):
            fetch(first_refs[other].at[low, far, inside], 0, other)
        for x in range(2):

            @pl.when(low == x)
            def _():
                for other in range(nodes):
                    fetch(second_refs[(other % 2) * 2 + x].at[other // 2, far, inside], 1, other)

        pltpu.make_async_copy(fitted_ref.at[left], left_buf.at[slot], load_sems.at[slot, 0]).start()
        for q in range(aux):
            pltpu.make_async_copy(
                fitted_ref.at[right, q], right_buf.at[slot, :, pl.ds(q * tile, tile)], load_sems.at[slot, 1]
            ).start()

    def wait_loads(slot):
        for k, buf in enumerate((left_buf, right_buf, tile_buf)):
            pltpu.make_async_copy(buf.at[slot], buf.at[slot], load_sems.at[slot, k]).wait()

    @pl.when(active > 0)
    def _():
        start_loads(0, 0)

    @pl.loop(0, slots)
    def _(s):
        total[s] = jnp.zeros(total.shape[1:], jnp.float32)

    def contract(first, second):
        return lax.dot_general(first, second, (((1,), (1,)), ((), ())), preferred_element_type=jnp.float32)

    @pl.loop(0, active)
    def _(i):
        slot = i % 2

        @pl.when(i + 1 < active)
        def _():
            start_loads(i + 1, 1 - slot)

        wait_loads(slot)
        a, b, _, _, _ = indices(work[i])
        straight = slot_of[a * side + b]
        crossed = slot_of[b * side + a]
        left_all = left_buf[slot].reshape(aux * tile, tile)
        for p in range(2):
            half = jnp.dot(left_all, tile_buf[slot, p], preferred_element_type=jnp.float32).astype(jnp.bfloat16)
            for q in range(aux):
                half_buf[p, :, q * tile:(q + 1) * tile] = half[q * tile:(q + 1) * tile]
        shape = total.shape[1:]
        total[straight] += contract(half_buf[0], right_buf[slot]).reshape(shape)
        total[crossed] += contract(right_buf[slot], half_buf[1]).reshape(shape)

    mine = node_index % 2
    stores = [
        pltpu.make_async_copy(total.at[:, :, mine], keep_ref, store_sems.at[0]),
        pltpu.make_async_copy(total.at[:, :, 1 - mine], send_ref, store_sems.at[1]),
    ]
    for copy in stores:
        copy.start()
    for copy in stores:
        copy.wait()


def ladder_terms(mask, tasks, owner_map, fitted, first, second, nodes, cores):
    tile_pairs, aux, tile, _ = fitted.shape
    slots_here, rows = first[0].shape[2:4]
    side = math.isqrt(tile_pairs)
    dims = (nodes, cores, slots_here, rows, tile, aux, tile_pairs, side)
    smem = pl.BlockSpec(memory_space=pltpu.SMEM)
    hbm = pl.BlockSpec(memory_space=pl.ANY)
    part = jax.ShapeDtypeStruct((tile_pairs, nodes // 2, rows, tile), jnp.float32)
    return pl.pallas_call(
        functools.partial(ladder_kernel, dims),
        out_shape=(part, part),
        in_specs=[smem, smem, smem] + [hbm] * (1 + len(first) + len(second)),
        out_specs=(hbm, hbm),
        scratch_shapes=[
            pltpu.VMEM((2, aux, tile, tile), jnp.bfloat16),
            pltpu.VMEM((2, tile, aux * tile), jnp.bfloat16),
            pltpu.VMEM((2, tile, aux * tile), jnp.bfloat16),
            pltpu.VMEM((2, 2, tile, tile), jnp.bfloat16),
            pltpu.VMEM((tile_pairs, nodes // 2, 2, rows, tile), jnp.float32),
            pltpu.SMEM((tasks.shape[0] + 1,), jnp.int32),
            pltpu.SMEM((tile_pairs,), jnp.int32),
            pltpu.SemaphoreType.DMA((2, 3)),
            pltpu.SemaphoreType.DMA((2,)),
        ],
        compiler_params=pltpu.CompilerParams(vmem_limit_bytes=32 * 1024 * 1024),
        cost_estimate=pl.CostEstimate(flops=20 * 10**9, bytes_accessed=30 * 2**20, transcendentals=0),
        name="ladder",
    )(mask, tasks, owner_map, fitted, *first, *second)


def swap(array, mask, total):
    return lax.ppermute(array, AXES, [(i, i ^ mask) for i in range(total)])


def pick(array, index, axis):
    return lax.dynamic_index_in_dim(array, index, axis, keepdims=False)


def halve(value, index, axis, mask, total):
    shape = value.shape
    split = value.reshape(shape[:axis] + (shape[axis] // 2, 2) + shape[axis + 1:])
    other = swap(pick(split, 1 - index, axis + 1), mask, total)
    own = pick(split, index, axis + 1)
    return (own.astype(jnp.float32) + other.astype(jnp.float32)).astype(value.dtype)


def add_other_core(keep, send, nodes, cores, scale):
    got = swap(send, cores, nodes * cores)
    slots, inner, rows, tile = keep.shape
    part = ((keep + got) * scale).astype(jnp.float16).reshape(cores, slots // cores, inner, rows, tile)
    return part[:, :, :, :rows // 2], part[:, :, :, rows // 2:]


def over_inner(value, nodes, cores):
    mask, index = 2 * cores, lax.axis_index("node") // 2
    while value.shape[2] > 1:
        value = halve(value, index % 2, 2, mask, nodes * cores)
        mask, index = mask * 2, index // 2
    return value


def over_low(value, nodes, cores):
    return halve(value, lax.axis_index("cores") % 2, 0, 1, nodes * cores)


def over_far(upper, lower, nodes, cores, scale):
    part = jnp.concatenate([upper, lower], axis=3)[:, :, 0]
    at = lax.axis_index("cores") // 2
    mine = pick(part, at, 0).astype(jnp.float32)
    for step in range(1, part.shape[0]):
        mine = mine + swap(pick(part, at ^ step, 0), 2 * step, nodes * cores).astype(jnp.float32)
    return mine * (0.5 / scale)


def pair_groups(partner_ref, pairs):
    count = jnp.int32(0)
    chosen = [jnp.int32(0)] * (pairs // 2)
    for p in range(pairs):
        is_rep = p < partner_ref[p]
        chosen = [jnp.where(is_rep & (count == g), p, old) for g, old in enumerate(chosen)]
        count = count + is_rep.astype(jnp.int32)
    return [(p, partner_ref[p]) for p in chosen]


def lower_kernel(partner_ref, amps_ref, *out_refs):
    for out_ref, both in zip(out_refs, pair_groups(partner_ref, amps_ref.shape[1])):
        for role, p in enumerate(both):
            out_ref[role] = amps_ref[:, p].astype(jnp.bfloat16)


def lower(partner, amplitudes):
    slots_here, pairs, rows, tile = amplitudes.shape
    vmem = pl.BlockSpec(memory_space=pltpu.VMEM)
    return pl.pallas_call(
        lower_kernel,
        out_shape=(jax.ShapeDtypeStruct((2, slots_here, rows, tile), jnp.bfloat16),) * (pairs // 2),
        in_specs=[pl.BlockSpec(memory_space=pltpu.SMEM), vmem],
        out_specs=(vmem,) * (pairs // 2),
        name="lower",
    )(partner, amplitudes)


def spread_far(part, cores, total):
    return [part] + [swap(part, 2 * step, total) for step in range(1, cores // 2)]


def spread_inner(parts, nodes, cores):
    total = nodes * cores
    first = jnp.stack([part[0] for part in parts])
    first = jnp.stack([first, swap(first, 1, total)])
    pieces = {0: jnp.stack([part[1] for part in parts])}
    bit = nodes // 2
    while bit > 1:
        pieces.update({other | bit: swap(piece, bit * cores, total) for other, piece in pieces.items()})
        bit //= 2
    return first, jnp.stack([pieces[2 * upper] for upper in range(nodes // 2)])


def spread_outer(first, second, nodes, cores):
    total = nodes * cores
    pieces = {0: first}
    bit = nodes // 2
    while bit > 1:
        pieces.update({other | bit: swap(piece, bit * cores, total) for other, piece in pieces.items()})
        bit //= 2
    return [pieces[2 * upper] for upper in range(1, nodes // 2)], swap(second, 1, total)


def spread_last(first, second, nodes, cores):
    total = nodes * cores
    return [swap(piece, cores, total) for piece in first], [swap(piece, cores, total) for piece in second]


def turn_blocks(mine, nodes, cores, scale):
    total = nodes * cores
    slots_here, rows, tile = mine.shape
    node_index = lax.axis_index("node")
    turned = (mine * scale).astype(jnp.float16).reshape(slots_here * rows, tile).T
    turned = turned.reshape(nodes, rows, slots_here * rows)
    pieces = [pick(turned, node_index, 0)]
    pieces += [swap(pick(turned, node_index ^ step, 0), step * cores, total) for step in range(1, nodes)]
    pieces = jnp.stack(pieces)
    block = jnp.stack([pick(pieces, node_index ^ n, 0) for n in range(nodes)])
    return block.reshape(nodes, rows, slots_here, rows).transpose(2, 1, 0, 3).reshape(slots_here, rows, tile)


def every_block(near, nodes, cores, scale):
    every = jnp.stack([near, swap(near, 1, nodes * cores)], axis=1)
    return every.reshape((cores,) + near.shape[1:]).astype(jnp.float32) * (1.0 / scale)


def update_kernel(side, owner_ref, partner_ref, pair_ref, energy_ref, column_ref, amps_ref, *refs):
    slots_here, pairs, rows, tile = amps_ref.shape
    groups = pairs // 2
    straight, crossed, out_ref, slot_of = refs[:groups], refs[groups:2 * groups], refs[-2], refs[-1]
    node_index = lax.axis_index("node")
    core_index = lax.axis_index("cores")

    def invert(s, carry):
        slot_of[owner_ref[s]] = s
        return carry

    lax.fori_loop(0, owner_ref.shape[0], invert, 0)
    for j in range(slots_here):
        mine = owner_ref[core_index * slots_here + j]
        row_tile, col_tile = mine // side, mine % side
        place = slot_of[col_tile * side + row_tile]
        apart, inside = (place // slots_here) ^ core_index, place % slots_here
        row_energy = energy_ref[pl.ds(pl.multiple_of(row_tile * tile + node_index * rows, 8), rows), :]
        col_energy = column_ref[pl.ds(col_tile, 1), :]
        for g, (rep, twin) in enumerate(pair_groups(partner_ref, pairs)):
            for p, value in ((rep, straight[g][j]), (twin, crossed[g][apart, inside])):
                denominator = (pair_ref[p] - row_energy) - col_energy
                out_ref[j, p] = amps_ref[j, p] + value / denominator


def update(owner_map, partner, pair_energy, virt_energy, amplitudes, straight, crossed):
    tile = amplitudes.shape[3]
    smem = pl.BlockSpec(memory_space=pltpu.SMEM)
    vmem = pl.BlockSpec(memory_space=pltpu.VMEM)
    return pl.pallas_call(
        functools.partial(update_kernel, math.isqrt(owner_map.shape[0])),
        out_shape=jax.ShapeDtypeStruct(amplitudes.shape, jnp.float32),
        in_specs=[smem] * 3 + [vmem] * (3 + len(straight) + len(crossed)),
        out_specs=vmem,
        scratch_shapes=[pltpu.SMEM(owner_map.shape, jnp.int32)],
        compiler_params=pltpu.CompilerParams(vmem_limit_bytes=32 * 1024 * 1024),
        name="update",
    )(
        owner_map, partner, pair_energy, virt_energy.reshape(-1, 1), virt_energy.reshape(-1, tile),
        amplitudes, *straight, *crossed,
    )


def body(nodes, cores, fitted, fit_mask, tasks, owner_map, partner, amplitudes, pair_energy, virt_energy):
    scale = 2.0 ** -9
    total = nodes * cores
    parts = lower(partner, amplitudes)
    groups = len(parts)
    barrier = lax.optimization_barrier

    far, inner, outer = [], [], []
    for g in range(groups):
        part = parts[g]
        if g:
            part, far[g - 1] = barrier((part, far[g - 1]))
        far.append(spread_far(part, cores, total))
    for g in range(groups):
        inner.append(spread_inner(far[g], nodes, cores))
        outer.append(spread_outer(*inner[g], nodes, cores))
    sums = []
    for g in range(groups):
        first = [inner[g][0]] + outer[g][0]
        second = [inner[g][1], outer[g][1]]
        if g:
            (first, second), sums[g - 1] = barrier(((first, second), sums[g - 1]))
        first_far, second_far = spread_last(first, second, nodes, cores)
        first = [piece for pair in zip(first, first_far) for piece in pair]
        sums.append(ladder_terms(fit_mask, tasks, owner_map, fitted, first, second + second_far, nodes, cores))
    stages = [
        lambda v: add_other_core(*v, nodes, cores, scale),
        lambda v: (over_inner(v[0], nodes, cores), over_low(v[1], nodes, cores)),
        lambda v: (over_low(v[0], nodes, cores), over_inner(v[1], nodes, cores)),
        lambda v: over_far(*v, nodes, cores, scale),
        lambda v: turn_blocks(v, nodes, cores, scale),
        lambda v: jnp.stack(spread_far(v, cores, total)),
        lambda v: every_block(v, nodes, cores, scale),
    ]
    state, straight = list(sums), [None] * groups
    for step in range(len(stages) + groups - 1):
        live = [g for g in range(groups) if 0 <= step - g < len(stages)]
        for g in live:
            state[g] = stages[step - g](state[g])
            if step - g == 3:
                straight[g] = state[g]
        upcoming = [g for g in range(groups) if 0 <= step + 1 - g < len(stages)]
        if len(upcoming) > 1 and step:
            tied = barrier(tuple(state[g] for g in upcoming))
            for g, value in zip(upcoming, tied):
                state[g] = value
    crossed = state
    return update(owner_map, partner, pair_energy, virt_energy, amplitudes, straight, crossed)


def solution(mesh):
    placed = (P(None, AXES, None, None), P(), P(), P(), P(), P("cores", None, "node", None), P(), P())
    return jax.shard_map(
        functools.partial(body, mesh.shape["node"], mesh.shape["cores"]),
        mesh=mesh, in_specs=placed, out_specs=P("cores", None, "node", None), check_vma=False,
    )
```

```python
import functools
import math

import jax
import jax.numpy as jnp
from jax import lax
from jax.experimental import pallas as pl
from jax.experimental.pallas import tpu as pltpu
from jax.sharding import PartitionSpec as P

AXES = ("node", "cores")


def ladder_kernel(dims, mask_ref, tasks_ref, owner_ref, fitted_ref, *refs):
    nodes, cores, slots_here, rows, tile, aux, slots, side = dims
    amps_refs, refs = refs[:-11], refs[-11:]
    keep_ref, send_ref, left_buf, right_buf, half_buf, tile_buf, total, work, slot_of, load_sems, store_sems = refs
    task_count = tasks_ref.shape[0]
    node_index = lax.axis_index("node")
    core_index = lax.axis_index("cores")
    block = node_index * cores + core_index

    def invert(s, carry):
        slot_of[owner_ref[s]] = s
        return carry

    lax.fori_loop(0, slots, invert, 0)

    def indices(t):
        out_tile = tasks_ref[t, 0]
        in_tile = tasks_ref[t, 1]
        a, b = out_tile // side, out_tile % side
        c, d = in_tile // side, in_tile % side
        return a, b, a * side + c, b * side + d, in_tile

    def enlist(t, count):
        _, _, left, right, _ = indices(t)
        work[count] = t
        return count + mask_ref[left, block] * mask_ref[right, block]

    active = lax.fori_loop(0, task_count, enlist, jnp.int32(0))

    def start_loads(i, slot):
        _, _, left, right, in_tile = indices(work[i])
        place = slot_of[in_tile]
        inside = place % slots_here
        owner = place // slots_here
        apart = owner ^ core_index
        low, far = apart % 2, apart // 2

        def fetch(source, role, node):
            strip = pl.ds(pl.multiple_of(node * rows, rows), rows)
            pltpu.make_async_copy(source, tile_buf.at[slot, role, strip, :], load_sems.at[slot, 2]).start()

        if len(amps_refs) == 1:
            for node in range(nodes):
                fetch(amps_refs[0].at[node * cores + owner, :, inside], slice(None), node)
        else:
            first_refs, second_refs = amps_refs[:nodes], amps_refs[nodes:]
            for other in range(nodes):
                fetch(first_refs[other].at[low, far, inside], 0, node_index ^ other)
            for x in range(2):

                @pl.when(low == x)
                def _():
                    for other in range(nodes):
                        source = second_refs[(other % 2) * 2 + x].at[other // 2, far, inside]
                        fetch(source, 1, node_index ^ other)

        pltpu.make_async_copy(fitted_ref.at[left], left_buf.at[slot], load_sems.at[slot, 0]).start()
        for q in range(aux):
            pltpu.make_async_copy(
                fitted_ref.at[right, q], right_buf.at[slot, :, pl.ds(q * tile, tile)], load_sems.at[slot, 1]
            ).start()

    def wait_loads(slot):
        for k, buf in enumerate((left_buf, right_buf, tile_buf)):
            pltpu.make_async_copy(buf.at[slot], buf.at[slot], load_sems.at[slot, k]).wait()

    @pl.when(active > 0)
    def _():
        start_loads(0, 0)

    @pl.loop(0, slots)
    def _(s):
        total[s] = jnp.zeros(total.shape[1:], jnp.float32)

    def contract(first, second):
        return lax.dot_general(first, second, (((1,), (1,)), ((), ())), preferred_element_type=jnp.float32)

    @pl.loop(0, active)
    def _(i):
        slot = i % 2

        @pl.when(i + 1 < active)
        def _():
            start_loads(i + 1, 1 - slot)

        wait_loads(slot)
        a, b, _, _, _ = indices(work[i])
        straight = slot_of[a * side + b]
        crossed = slot_of[b * side + a]
        left_all = left_buf[slot].reshape(aux * tile, tile)
        for p in range(2):
            half = jnp.dot(left_all, tile_buf[slot, p], preferred_element_type=jnp.float32).astype(jnp.bfloat16)
            for q in range(aux):
                half_buf[p, :, q * tile:(q + 1) * tile] = half[q * tile:(q + 1) * tile]
        shape = total.shape[1:]
        total[straight] += contract(half_buf[0], right_buf[slot]).reshape(shape)
        total[crossed] += contract(right_buf[slot], half_buf[1]).reshape(shape)

    mine = node_index % 2
    stores = [
        pltpu.make_async_copy(total.at[:, :, mine], keep_ref, store_sems.at[0]),
        pltpu.make_async_copy(total.at[:, :, 1 - mine], send_ref, store_sems.at[1]),
    ]
    for copy in stores:
        copy.start()
    for copy in stores:
        copy.wait()


def ladder_terms(mask, tasks, owner_map, fitted, amps, nodes, cores):
    tile_pairs, aux, tile, _ = fitted.shape
    slots_here, rows = tile_pairs // cores, tile // nodes
    side = math.isqrt(tile_pairs)
    dims = (nodes, cores, slots_here, rows, tile, aux, tile_pairs, side)
    smem = pl.BlockSpec(memory_space=pltpu.SMEM)
    hbm = pl.BlockSpec(memory_space=pl.ANY)
    part = jax.ShapeDtypeStruct((tile_pairs, nodes // 2, rows, tile), jnp.float32)
    return pl.pallas_call(
        functools.partial(ladder_kernel, dims),
        out_shape=(part, part),
        in_specs=[smem, smem, smem] + [hbm] * (1 + len(amps)),
        out_specs=(hbm, hbm),
        scratch_shapes=[
            pltpu.VMEM((2, aux, tile, tile), jnp.bfloat16),
            pltpu.VMEM((2, tile, aux * tile), jnp.bfloat16),
            pltpu.VMEM((2, tile, aux * tile), jnp.bfloat16),
            pltpu.VMEM((2, 2, tile, tile), jnp.bfloat16),
            pltpu.VMEM((tile_pairs, nodes // 2, 2, rows, tile), jnp.float32),
            pltpu.SMEM((tasks.shape[0] + 1,), jnp.int32),
            pltpu.SMEM((tile_pairs,), jnp.int32),
            pltpu.SemaphoreType.DMA((2, 3)),
            pltpu.SemaphoreType.DMA((2,)),
        ],
        compiler_params=pltpu.CompilerParams(vmem_limit_bytes=32 * 1024 * 1024),
        cost_estimate=pl.CostEstimate(flops=20 * 10**9, bytes_accessed=30 * 2**20, transcendentals=0),
        name="ladder",
    )(mask, tasks, owner_map, fitted, *amps)


def swap(array, mask, total):
    return lax.ppermute(array, AXES, [(i, i ^ mask) for i in range(total)])


def pick(array, index, axis):
    return lax.dynamic_index_in_dim(array, index, axis, keepdims=False)


def halve(value, index, axis, mask, total):
    shape = value.shape
    split = value.reshape(shape[:axis] + (shape[axis] // 2, 2) + shape[axis + 1:])
    other = swap(pick(split, 1 - index, axis + 1), mask, total)
    own = pick(split, index, axis + 1)
    return (own.astype(jnp.float32) + other.astype(jnp.float32)).astype(value.dtype)


def add_other_core(keep, send, nodes, cores, scale):
    got = swap(send, cores, nodes * cores)
    slots, inner, rows, tile = keep.shape
    part = ((keep + got) * scale).astype(jnp.float16).reshape(cores, slots // cores, inner, rows, tile)
    return part[:, :, :, :rows // 2], part[:, :, :, rows // 2:]


def over_inner(value, nodes, cores):
    mask, index = 2 * cores, lax.axis_index("node") // 2
    while value.shape[2] > 1:
        value = halve(value, index % 2, 2, mask, nodes * cores)
        mask, index = mask * 2, index // 2
    return value


def over_low(value, nodes, cores):
    return halve(value, lax.axis_index("cores") % 2, 0, 1, nodes * cores)


def over_far(upper, lower, nodes, cores, scale):
    part = jnp.concatenate([upper, lower], axis=3)[:, :, 0]
    at = lax.axis_index("cores") // 2
    mine = pick(part, at, 0).astype(jnp.float32)
    for step in range(1, part.shape[0]):
        mine = mine + swap(pick(part, at ^ step, 0), 2 * step, nodes * cores).astype(jnp.float32)
    return mine * (0.5 / scale)


def pair_groups(partner_ref, pairs):
    count = jnp.int32(0)
    chosen = [jnp.int32(0)] * (pairs // 2)
    for p in range(pairs):
        is_rep = p < partner_ref[p]
        chosen = [jnp.where(is_rep & (count == g), p, old) for g, old in enumerate(chosen)]
        count = count + is_rep.astype(jnp.int32)
    return [(p, partner_ref[p]) for p in chosen]


def lower_kernel(partner_ref, amps_ref, *out_refs):
    for out_ref, both in zip(out_refs, pair_groups(partner_ref, amps_ref.shape[1])):
        for role, p in enumerate(both):
            out_ref[role] = amps_ref[:, p].astype(jnp.bfloat16)


def lower(partner, amplitudes):
    slots_here, pairs, rows, tile = amplitudes.shape
    vmem = pl.BlockSpec(memory_space=pltpu.VMEM)
    return pl.pallas_call(
        lower_kernel,
        out_shape=(jax.ShapeDtypeStruct((2, slots_here, rows, tile), jnp.bfloat16),) * (pairs // 2),
        in_specs=[pl.BlockSpec(memory_space=pltpu.SMEM), vmem],
        out_specs=(vmem,) * (pairs // 2),
        name="lower",
    )(partner, amplitudes)


def spread_far(part, cores, total):
    return [part] + [swap(part, 2 * step, total) for step in range(1, cores // 2)]


def spread_inner(parts, nodes, cores):
    total = nodes * cores
    first = jnp.stack([part[0] for part in parts])
    first = jnp.stack([first, swap(first, 1, total)])
    pieces = {0: jnp.stack([part[1] for part in parts])}
    bit = nodes // 2
    while bit > 1:
        pieces.update({other | bit: swap(piece, bit * cores, total) for other, piece in pieces.items()})
        bit //= 2
    return first, jnp.stack([pieces[2 * upper] for upper in range(nodes // 2)])


def spread_outer(first, second, nodes, cores):
    total = nodes * cores
    pieces = {0: first}
    bit = nodes // 2
    while bit > 1:
        pieces.update({other | bit: swap(piece, bit * cores, total) for other, piece in pieces.items()})
        bit //= 2
    return [pieces[2 * upper] for upper in range(1, nodes // 2)], swap(second, 1, total)


def spread_last(first, second, nodes, cores):
    total = nodes * cores
    return [swap(piece, cores, total) for piece in first], [swap(piece, cores, total) for piece in second]


def turn_blocks(mine, nodes, cores, scale):
    total = nodes * cores
    slots_here, rows, tile = mine.shape
    node_index = lax.axis_index("node")
    turned = (mine * scale).astype(jnp.float16).reshape(slots_here * rows, tile).T
    turned = turned.reshape(nodes, rows, slots_here * rows)
    pieces = [pick(turned, node_index, 0)]
    pieces += [swap(pick(turned, node_index ^ step, 0), step * cores, total) for step in range(1, nodes)]
    pieces = jnp.stack(pieces)
    block = jnp.stack([pick(pieces, node_index ^ n, 0) for n in range(nodes)])
    return block.reshape(nodes, rows, slots_here, rows).transpose(2, 1, 0, 3).reshape(slots_here, rows, tile)


def every_block(near, nodes, cores, scale):
    every = jnp.stack([near, swap(near, 1, nodes * cores)], axis=1)
    return every.reshape((cores,) + near.shape[1:]).astype(jnp.float32) * (1.0 / scale)


def update_kernel(side, owner_ref, partner_ref, pair_ref, energy_ref, column_ref, amps_ref, *refs):
    slots_here, pairs, rows, tile = amps_ref.shape
    groups = pairs // 2
    straight, crossed, out_ref, slot_of = refs[:groups], refs[groups:2 * groups], refs[-2], refs[-1]
    node_index = lax.axis_index("node")
    core_index = lax.axis_index("cores")

    def invert(s, carry):
        slot_of[owner_ref[s]] = s
        return carry

    lax.fori_loop(0, owner_ref.shape[0], invert, 0)
    for j in range(slots_here):
        mine = owner_ref[core_index * slots_here + j]
        row_tile, col_tile = mine // side, mine % side
        place = slot_of[col_tile * side + row_tile]
        apart, inside = (place // slots_here) ^ core_index, place % slots_here
        row_energy = energy_ref[pl.ds(pl.multiple_of(row_tile * tile + node_index * rows, 8), rows), :]
        col_energy = column_ref[pl.ds(col_tile, 1), :]
        for g, (rep, twin) in enumerate(pair_groups(partner_ref, pairs)):
            for p, value in ((rep, straight[g][j]), (twin, crossed[g][apart, inside])):
                denominator = (pair_ref[p] - row_energy) - col_energy
                out_ref[j, p] = amps_ref[j, p] + value / denominator


def update(owner_map, partner, pair_energy, virt_energy, amplitudes, straight, crossed):
    tile = amplitudes.shape[3]
    smem = pl.BlockSpec(memory_space=pltpu.SMEM)
    vmem = pl.BlockSpec(memory_space=pltpu.VMEM)
    return pl.pallas_call(
        functools.partial(update_kernel, math.isqrt(owner_map.shape[0])),
        out_shape=jax.ShapeDtypeStruct(amplitudes.shape, jnp.float32),
        in_specs=[smem] * 3 + [vmem] * (3 + len(straight) + len(crossed)),
        out_specs=vmem,
        scratch_shapes=[pltpu.SMEM(owner_map.shape, jnp.int32)],
        compiler_params=pltpu.CompilerParams(vmem_limit_bytes=32 * 1024 * 1024),
        name="update",
    )(
        owner_map, partner, pair_energy, virt_energy.reshape(-1, 1), virt_energy.reshape(-1, tile),
        amplitudes, *straight, *crossed,
    )


def body(nodes, cores, fitted, fit_mask, tasks, owner_map, partner, amplitudes, pair_energy, virt_energy):
    scale = 2.0 ** -9
    total = nodes * cores
    parts = lower(partner, amplitudes)
    groups = len(parts)

    amps = []
    for g in range(groups - 1):
        inner = spread_inner(spread_far(parts[g], cores, total), nodes, cores)
        outer = spread_outer(*inner, nodes, cores)
        first = [inner[0]] + outer[0]
        second = [inner[1], outer[1]]
        first_far, second_far = spread_last(first, second, nodes, cores)
        amps.append([piece for pair in zip(first, first_far) for piece in pair] + second + second_far)
    amps.append([lax.all_gather(parts[-1], AXES, axis=0, tiled=False)])
    sums = []
    for g in range(groups):
        sums.append(ladder_terms(fit_mask, tasks, owner_map, fitted, amps[g], nodes, cores))
    stages = [
        lambda v: add_other_core(*v, nodes, cores, scale),
        lambda v: (over_inner(v[0], nodes, cores), over_low(v[1], nodes, cores)),
        lambda v: (over_low(v[0], nodes, cores), over_inner(v[1], nodes, cores)),
        lambda v: over_far(*v, nodes, cores, scale),
        lambda v: turn_blocks(v, nodes, cores, scale),
        lambda v: jnp.stack(spread_far(v, cores, total)),
        lambda v: every_block(v, nodes, cores, scale),
    ]
    straight, crossed = [], []
    for value in sums:
        for step, stage in enumerate(stages):
            value = stage(value)
            if step == 3:
                straight.append(value)
        crossed.append(value)
    return update(owner_map, partner, pair_energy, virt_energy, amplitudes, straight, crossed)


def solution(mesh):
    placed = (P(None, AXES, None, None), P(), P(), P(), P(), P("cores", None, "node", None), P(), P())
    return jax.shard_map(
        functools.partial(body, mesh.shape["node"], mesh.shape["cores"]),
        mesh=mesh, in_specs=placed, out_specs=P("cores", None, "node", None), check_vma=False,
    )
```

```python
import functools
import math

import jax
import jax.numpy as jnp
from jax import lax
from jax.experimental import pallas as pl
from jax.experimental.pallas import tpu as pltpu
from jax.sharding import PartitionSpec as P

AXES = ("node", "cores")


def ladder_kernel(dims, mask_ref, tasks_ref, owner_ref, fitted_ref, *refs):
    nodes, cores, slots_here, rows, tile, aux, slots, side = dims
    amps_refs, refs = refs[:-11], refs[-11:]
    keep_ref, send_ref, left_buf, right_buf, half_buf, tile_buf, total, work, slot_of, load_sems, store_sems = refs
    task_count = tasks_ref.shape[0]
    node_index = lax.axis_index("node")
    core_index = lax.axis_index("cores")
    block = node_index * cores + core_index

    def invert(s, carry):
        slot_of[owner_ref[s]] = s
        return carry

    lax.fori_loop(0, slots, invert, 0)

    def indices(t):
        out_tile = tasks_ref[t, 0]
        in_tile = tasks_ref[t, 1]
        a, b = out_tile // side, out_tile % side
        c, d = in_tile // side, in_tile % side
        return a, b, a * side + c, b * side + d, in_tile

    def enlist(t, count):
        _, _, left, right, _ = indices(t)
        work[count] = t
        return count + mask_ref[left, block] * mask_ref[right, block]

    active = lax.fori_loop(0, task_count, enlist, jnp.int32(0))

    def start_loads(i, slot):
        _, _, left, right, in_tile = indices(work[i])
        place = slot_of[in_tile]
        inside = place % slots_here
        owner = place // slots_here
        apart = owner ^ core_index
        low, far = apart % 2, apart // 2

        def fetch(source, role, node):
            strip = pl.ds(pl.multiple_of(node * rows, rows), rows)
            pltpu.make_async_copy(source, tile_buf.at[slot, role, strip, :], load_sems.at[slot, 2]).start()

        if len(amps_refs) == 1:
            for node in range(nodes):
                fetch(amps_refs[0].at[node * cores + owner, :, inside], slice(None), node)
        else:
            first_refs, second_refs = amps_refs[:nodes], amps_refs[nodes:]
            for other in range(nodes):
                fetch(first_refs[other].at[low, far, inside], 0, node_index ^ other)
            for x in range(2):

                @pl.when(low == x)
                def _():
                    for other in range(nodes):
                        source = second_refs[(other % 2) * 2 + x].at[other // 2, far, inside]
                        fetch(source, 1, node_index ^ other)

        pltpu.make_async_copy(fitted_ref.at[left], left_buf.at[slot], load_sems.at[slot, 0]).start()
        for q in range(aux):
            pltpu.make_async_copy(
                fitted_ref.at[right, q], right_buf.at[slot, :, pl.ds(q * tile, tile)], load_sems.at[slot, 1]
            ).start()

    def wait_loads(slot):
        for k, buf in enumerate((left_buf, right_buf, tile_buf)):
            pltpu.make_async_copy(buf.at[slot], buf.at[slot], load_sems.at[slot, k]).wait()

    @pl.when(active > 0)
    def _():
        start_loads(0, 0)

    @pl.loop(0, slots)
    def _(s):
        total[s] = jnp.zeros(total.shape[1:], jnp.float32)

    def contract(first, second):
        return lax.dot_general(first, second, (((1,), (1,)), ((), ())), preferred_element_type=jnp.float32)

    @pl.loop(0, active)
    def _(i):
        slot = i % 2

        @pl.when(i + 1 < active)
        def _():
            start_loads(i + 1, 1 - slot)

        wait_loads(slot)
        a, b, _, _, _ = indices(work[i])
        straight = slot_of[a * side + b]
        crossed = slot_of[b * side + a]
        left_all = left_buf[slot].reshape(aux * tile, tile)
        for p in range(2):
            half = jnp.dot(left_all, tile_buf[slot, p], preferred_element_type=jnp.float32).astype(jnp.bfloat16)
            for q in range(aux):
                half_buf[p, :, q * tile:(q + 1) * tile] = half[q * tile:(q + 1) * tile]
        shape = total.shape[1:]
        total[straight] += contract(half_buf[0], right_buf[slot]).reshape(shape)
        total[crossed] += contract(right_buf[slot], half_buf[1]).reshape(shape)

    mine = node_index % 2
    stores = [
        pltpu.make_async_copy(total.at[:, :, mine], keep_ref, store_sems.at[0]),
        pltpu.make_async_copy(total.at[:, :, 1 - mine], send_ref, store_sems.at[1]),
    ]
    for copy in stores:
        copy.start()
    for copy in stores:
        copy.wait()


def ladder_terms(mask, tasks, owner_map, fitted, amps, nodes, cores):
    tile_pairs, aux, tile, _ = fitted.shape
    slots_here, rows = tile_pairs // cores, tile // nodes
    side = math.isqrt(tile_pairs)
    dims = (nodes, cores, slots_here, rows, tile, aux, tile_pairs, side)
    smem = pl.BlockSpec(memory_space=pltpu.SMEM)
    hbm = pl.BlockSpec(memory_space=pl.ANY)
    part = jax.ShapeDtypeStruct((tile_pairs, nodes // 2, rows, tile), jnp.float32)
    return pl.pallas_call(
        functools.partial(ladder_kernel, dims),
        out_shape=(part, part),
        in_specs=[smem, smem, smem] + [hbm] * (1 + len(amps)),
        out_specs=(hbm, hbm),
        scratch_shapes=[
            pltpu.VMEM((2, aux, tile, tile), jnp.bfloat16),
            pltpu.VMEM((2, tile, aux * tile), jnp.bfloat16),
            pltpu.VMEM((2, tile, aux * tile), jnp.bfloat16),
            pltpu.VMEM((2, 2, tile, tile), jnp.bfloat16),
            pltpu.VMEM((tile_pairs, nodes // 2, 2, rows, tile), jnp.float32),
            pltpu.SMEM((tasks.shape[0] + 1,), jnp.int32),
            pltpu.SMEM((tile_pairs,), jnp.int32),
            pltpu.SemaphoreType.DMA((2, 3)),
            pltpu.SemaphoreType.DMA((2,)),
        ],
        compiler_params=pltpu.CompilerParams(vmem_limit_bytes=58 * 1024 * 1024),
        cost_estimate=pl.CostEstimate(flops=20 * 10**9, bytes_accessed=30 * 2**20, transcendentals=0),
        name="ladder",
    )(mask, tasks, owner_map, fitted, *amps)


def swap(array, mask, total):
    return lax.ppermute(array, AXES, [(i, i ^ mask) for i in range(total)])


def pick(array, index, axis):
    return lax.dynamic_index_in_dim(array, index, axis, keepdims=False)


def halve(value, index, axis, mask, total):
    shape = value.shape
    split = value.reshape(shape[:axis] + (shape[axis] // 2, 2) + shape[axis + 1:])
    other = swap(pick(split, 1 - index, axis + 1), mask, total)
    own = pick(split, index, axis + 1)
    return (own.astype(jnp.float32) + other.astype(jnp.float32)).astype(value.dtype)


def add_other_core(keep, send, nodes, cores, scale):
    got = swap(send, cores, nodes * cores)
    slots, inner, rows, tile = keep.shape
    part = ((keep + got) * scale).astype(jnp.float16).reshape(cores, slots // cores, inner, rows, tile)
    return part[:, :, :, :rows // 2], part[:, :, :, rows // 2:]


def over_inner(value, nodes, cores):
    mask, index = 2 * cores, lax.axis_index("node") // 2
    while value.shape[2] > 1:
        value = halve(value, index % 2, 2, mask, nodes * cores)
        mask, index = mask * 2, index // 2
    return value


def over_low(value, nodes, cores):
    return halve(value, lax.axis_index("cores") % 2, 0, 1, nodes * cores)


def over_far(upper, lower, nodes, cores, scale):
    part = jnp.concatenate([upper, lower], axis=3)[:, :, 0]
    at = lax.axis_index("cores") // 2
    mine = pick(part, at, 0).astype(jnp.float32)
    for step in range(1, part.shape[0]):
        mine = mine + swap(pick(part, at ^ step, 0), 2 * step, nodes * cores).astype(jnp.float32)
    return mine * (0.5 / scale)


def pair_groups(partner_ref, pairs):
    count = jnp.int32(0)
    chosen = [jnp.int32(0)] * (pairs // 2)
    for p in range(pairs):
        is_rep = p < partner_ref[p]
        chosen = [jnp.where(is_rep & (count == g), p, old) for g, old in enumerate(chosen)]
        count = count + is_rep.astype(jnp.int32)
    return [(p, partner_ref[p]) for p in chosen]


def lower_kernel(partner_ref, amps_ref, *out_refs):
    for out_ref, both in zip(out_refs, pair_groups(partner_ref, amps_ref.shape[1])):
        for role, p in enumerate(both):
            out_ref[role] = amps_ref[:, p].astype(jnp.bfloat16)


def lower(partner, amplitudes):
    slots_here, pairs, rows, tile = amplitudes.shape
    vmem = pl.BlockSpec(memory_space=pltpu.VMEM)
    return pl.pallas_call(
        lower_kernel,
        out_shape=(jax.ShapeDtypeStruct((2, slots_here, rows, tile), jnp.bfloat16),) * (pairs // 2),
        in_specs=[pl.BlockSpec(memory_space=pltpu.SMEM), vmem],
        out_specs=(vmem,) * (pairs // 2),
        name="lower",
    )(partner, amplitudes)


def spread_far(part, cores, total):
    return [part] + [swap(part, 2 * step, total) for step in range(1, cores // 2)]


def spread_inner(parts, nodes, cores):
    total = nodes * cores
    first = jnp.stack([part[0] for part in parts])
    first = jnp.stack([first, swap(first, 1, total)])
    pieces = {0: jnp.stack([part[1] for part in parts])}
    bit = nodes // 2
    while bit > 1:
        pieces.update({other | bit: swap(piece, bit * cores, total) for other, piece in pieces.items()})
        bit //= 2
    return first, jnp.stack([pieces[2 * upper] for upper in range(nodes // 2)])


def spread_outer(first, second, nodes, cores):
    total = nodes * cores
    pieces = {0: first}
    bit = nodes // 2
    while bit > 1:
        pieces.update({other | bit: swap(piece, bit * cores, total) for other, piece in pieces.items()})
        bit //= 2
    return [pieces[2 * upper] for upper in range(1, nodes // 2)], swap(second, 1, total)


def spread_last(first, second, nodes, cores):
    total = nodes * cores
    return [swap(piece, cores, total) for piece in first], [swap(piece, cores, total) for piece in second]


def turn_blocks(mine, nodes, cores, scale):
    total = nodes * cores
    slots_here, rows, tile = mine.shape
    node_index = lax.axis_index("node")
    turned = (mine * scale).astype(jnp.float16).reshape(slots_here * rows, tile).T
    turned = turned.reshape(nodes, rows, slots_here * rows)
    pieces = [pick(turned, node_index, 0)]
    pieces += [swap(pick(turned, node_index ^ step, 0), step * cores, total) for step in range(1, nodes)]
    pieces = jnp.stack(pieces)
    block = jnp.stack([pick(pieces, node_index ^ n, 0) for n in range(nodes)])
    return block.reshape(nodes, rows, slots_here, rows).transpose(2, 1, 0, 3).reshape(slots_here, rows, tile)


def every_block(near, nodes, cores, scale):
    every = jnp.stack([near, swap(near, 1, nodes * cores)], axis=1)
    return every.reshape((cores,) + near.shape[1:]).astype(jnp.float32) * (1.0 / scale)


def update_kernel(side, owner_ref, partner_ref, pair_ref, energy_ref, column_ref, amps_ref, *refs):
    slots_here, pairs, rows, tile = amps_ref.shape
    groups = pairs // 2
    straight, crossed, out_ref, slot_of = refs[:groups], refs[groups:2 * groups], refs[-2], refs[-1]
    node_index = lax.axis_index("node")
    core_index = lax.axis_index("cores")

    def invert(s, carry):
        slot_of[owner_ref[s]] = s
        return carry

    lax.fori_loop(0, owner_ref.shape[0], invert, 0)
    for j in range(slots_here):
        mine = owner_ref[core_index * slots_here + j]
        row_tile, col_tile = mine // side, mine % side
        place = slot_of[col_tile * side + row_tile]
        apart, inside = (place // slots_here) ^ core_index, place % slots_here
        row_energy = energy_ref[pl.ds(pl.multiple_of(row_tile * tile + node_index * rows, 8), rows), :]
        col_energy = column_ref[pl.ds(col_tile, 1), :]
        for g, (rep, twin) in enumerate(pair_groups(partner_ref, pairs)):
            for p, value in ((rep, straight[g][j]), (twin, crossed[g][apart, inside])):
                denominator = (pair_ref[p] - row_energy) - col_energy
                out_ref[j, p] = amps_ref[j, p] + value / denominator


def update(owner_map, partner, pair_energy, virt_energy, amplitudes, straight, crossed):
    tile = amplitudes.shape[3]
    smem = pl.BlockSpec(memory_space=pltpu.SMEM)
    vmem = pl.BlockSpec(memory_space=pltpu.VMEM)
    return pl.pallas_call(
        functools.partial(update_kernel, math.isqrt(owner_map.shape[0])),
        out_shape=jax.ShapeDtypeStruct(amplitudes.shape, jnp.float32),
        in_specs=[smem] * 3 + [vmem] * (3 + len(straight) + len(crossed)),
        out_specs=vmem,
        scratch_shapes=[pltpu.SMEM(owner_map.shape, jnp.int32)],
        compiler_params=pltpu.CompilerParams(vmem_limit_bytes=32 * 1024 * 1024),
        name="update",
    )(
        owner_map, partner, pair_energy, virt_energy.reshape(-1, 1), virt_energy.reshape(-1, tile),
        amplitudes, *straight, *crossed,
    )


def body(nodes, cores, fitted, fit_mask, tasks, owner_map, partner, amplitudes, pair_energy, virt_energy):
    scale = 2.0 ** -9
    total = nodes * cores
    parts = lower(partner, amplitudes)
    groups = len(parts)
    barrier = lax.optimization_barrier

    amps = []
    for g in range(groups - 1):
        inner = spread_inner(spread_far(parts[g], cores, total), nodes, cores)
        outer = spread_outer(*inner, nodes, cores)
        first = [inner[0]] + outer[0]
        second = [inner[1], outer[1]]
        first_far, second_far = spread_last(first, second, nodes, cores)
        amps.append([piece for pair in zip(first, first_far) for piece in pair] + second + second_far)
    amps.append([lax.all_gather(parts[-1], AXES, axis=0, tiled=False)])
    sums = []
    for g in range(groups):
        sums.append(ladder_terms(fit_mask, tasks, owner_map, fitted, amps[g], nodes, cores))
    stages = [
        lambda v: add_other_core(*v, nodes, cores, scale),
        lambda v: barrier((over_inner(v[0], nodes, cores), over_low(v[1], nodes, cores))),
        lambda v: barrier((over_low(v[0], nodes, cores), over_inner(v[1], nodes, cores))),
        lambda v: over_far(*v, nodes, cores, scale),
        lambda v: turn_blocks(v, nodes, cores, scale),
        lambda v: jnp.stack(spread_far(v, cores, total)),
        lambda v: every_block(v, nodes, cores, scale),
    ]
    results = []
    for g in range(groups):
        results.append([sums[g]])
    for step in range(len(stages) + groups - 1):
        for g in reversed(range(groups)):
            stage = step - g
            if not 0 <= stage < len(stages):
                continue
            value = results[g][stage]
            if stage and g + 1 < groups and len(results[g + 1]) > 1:
                value = barrier((value, results[g + 1][-1]))[0]
            results[g].append(stages[stage](value))
    straight = [values[4] for values in results]
    crossed = [values[-1] for values in results]
    return update(owner_map, partner, pair_energy, virt_energy, amplitudes, straight, crossed)


def solution(mesh):
    placed = (P(None, AXES, None, None), P(), P(), P(), P(), P("cores", None, "node", None), P(), P())
    return jax.shard_map(
        functools.partial(body, mesh.shape["node"], mesh.shape["cores"]),
        mesh=mesh, in_specs=placed, out_specs=P("cores", None, "node", None), check_vma=False,
    )
```

```python
import functools
import math

import jax
import jax.numpy as jnp
from jax import lax
from jax.experimental import pallas as pl
from jax.experimental.pallas import tpu as pltpu
from jax.sharding import PartitionSpec as P

AXES = ("node", "cores")


def ladder_kernel(dims, mask_ref, tasks_ref, owner_ref, fitted_ref, *refs):
    nodes, cores, slots_here, rows, tile, aux, slots, side = dims
    amps_refs, refs = refs[:-11], refs[-11:]
    keep_ref, send_ref, left_buf, right_buf, half_buf, tile_buf, total, work, slot_of, load_sems, store_sems = refs
    task_count = tasks_ref.shape[0]
    node_index = lax.axis_index("node")
    core_index = lax.axis_index("cores")
    block = node_index * cores + core_index

    def invert(s, carry):
        slot_of[owner_ref[s]] = s
        return carry

    lax.fori_loop(0, slots, invert, 0)

    def indices(t):
        out_tile = tasks_ref[t, 0]
        in_tile = tasks_ref[t, 1]
        a, b = out_tile // side, out_tile % side
        c, d = in_tile // side, in_tile % side
        return a, b, a * side + c, b * side + d, in_tile

    def enlist(t, count):
        _, _, left, right, _ = indices(t)
        work[count] = t
        return count + mask_ref[left, block] * mask_ref[right, block]

    active = lax.fori_loop(0, task_count, enlist, jnp.int32(0))

    def start_loads(i, slot):
        _, _, left, right, in_tile = indices(work[i])
        place = slot_of[in_tile]
        inside = place % slots_here
        owner = place // slots_here
        apart = owner ^ core_index
        low, far = apart % 2, apart // 2

        def fetch(source, role, node):
            strip = pl.ds(pl.multiple_of(node * rows, rows), rows)
            pltpu.make_async_copy(source, tile_buf.at[slot, role, strip, :], load_sems.at[slot, 2]).start()

        if len(amps_refs) == 1:
            for node in range(nodes):
                fetch(amps_refs[0].at[node * cores + owner, :, inside], slice(None), node)
        else:
            first_refs, second_refs = amps_refs[:nodes], amps_refs[nodes:]
            for other in range(nodes):
                fetch(first_refs[other].at[low, far, inside], 0, node_index ^ other)
            for x in range(2):

                @pl.when(low == x)
                def _():
                    for other in range(nodes):
                        source = second_refs[(other % 2) * 2 + x].at[other // 2, far, inside]
                        fetch(source, 1, node_index ^ other)

        pltpu.make_async_copy(fitted_ref.at[left], left_buf.at[slot], load_sems.at[slot, 0]).start()
        for q in range(aux):
            pltpu.make_async_copy(
                fitted_ref.at[right, q], right_buf.at[slot, :, pl.ds(q * tile, tile)], load_sems.at[slot, 1]
            ).start()

    def wait_loads(slot):
        for k, buf in enumerate((left_buf, right_buf, tile_buf)):
            pltpu.make_async_copy(buf.at[slot], buf.at[slot], load_sems.at[slot, k]).wait()

    @pl.when(active > 0)
    def _():
        start_loads(0, 0)

    @pl.loop(0, slots)
    def _(s):
        total[s] = jnp.zeros(total.shape[1:], jnp.float32)

    def contract(first, second):
        return lax.dot_general(first, second, (((1,), (1,)), ((), ())), preferred_element_type=jnp.float32)

    @pl.loop(0, active)
    def _(i):
        slot = i % 2

        @pl.when(i + 1 < active)
        def _():
            start_loads(i + 1, 1 - slot)

        wait_loads(slot)
        a, b, _, _, _ = indices(work[i])
        straight = slot_of[a * side + b]
        crossed = slot_of[b * side + a]
        left_all = left_buf[slot].reshape(aux * tile, tile)
        for p in range(2):
            half = jnp.dot(left_all, tile_buf[slot, p], preferred_element_type=jnp.float32).astype(jnp.bfloat16)
            for q in range(aux):
                half_buf[p, :, q * tile:(q + 1) * tile] = half[q * tile:(q + 1) * tile]
        shape = total.shape[1:]
        total[straight] += contract(half_buf[0], right_buf[slot]).reshape(shape)
        total[crossed] += contract(right_buf[slot], half_buf[1]).reshape(shape)

    mine = node_index % 2
    stores = [
        pltpu.make_async_copy(total.at[:, :, mine], keep_ref, store_sems.at[0]),
        pltpu.make_async_copy(total.at[:, :, 1 - mine], send_ref, store_sems.at[1]),
    ]
    for copy in stores:
        copy.start()
    for copy in stores:
        copy.wait()


def ladder_terms(mask, tasks, owner_map, fitted, amps, nodes, cores):
    tile_pairs, aux, tile, _ = fitted.shape
    slots_here, rows = tile_pairs // cores, tile // nodes
    side = math.isqrt(tile_pairs)
    dims = (nodes, cores, slots_here, rows, tile, aux, tile_pairs, side)
    smem = pl.BlockSpec(memory_space=pltpu.SMEM)
    hbm = pl.BlockSpec(memory_space=pl.ANY)
    part = jax.ShapeDtypeStruct((tile_pairs, nodes // 2, rows, tile), jnp.float32)
    return pl.pallas_call(
        functools.partial(ladder_kernel, dims),
        out_shape=(part, part),
        in_specs=[smem, smem, smem] + [hbm] * (1 + len(amps)),
        out_specs=(hbm, hbm),
        scratch_shapes=[
            pltpu.VMEM((2, aux, tile, tile), jnp.bfloat16),
            pltpu.VMEM((2, tile, aux * tile), jnp.bfloat16),
            pltpu.VMEM((2, tile, aux * tile), jnp.bfloat16),
            pltpu.VMEM((2, 2, tile, tile), jnp.bfloat16),
            pltpu.VMEM((tile_pairs, nodes // 2, 2, rows, tile), jnp.float32),
            pltpu.SMEM((tasks.shape[0] + 1,), jnp.int32),
            pltpu.SMEM((tile_pairs,), jnp.int32),
            pltpu.SemaphoreType.DMA((2, 3)),
            pltpu.SemaphoreType.DMA((2,)),
        ],
        compiler_params=pltpu.CompilerParams(vmem_limit_bytes=58 * 1024 * 1024),
        cost_estimate=pl.CostEstimate(flops=20 * 10**9, bytes_accessed=30 * 2**20, transcendentals=0),
        name="ladder",
    )(mask, tasks, owner_map, fitted, *amps)


def swap(array, mask, total):
    return lax.ppermute(array, AXES, [(i, i ^ mask) for i in range(total)])


def pick(array, index, axis):
    return lax.dynamic_index_in_dim(array, index, axis, keepdims=False)


def halve(value, index, axis, mask, total):
    shape = value.shape
    split = value.reshape(shape[:axis] + (shape[axis] // 2, 2) + shape[axis + 1:])
    other = swap(pick(split, 1 - index, axis + 1), mask, total)
    own = pick(split, index, axis + 1)
    return (own.astype(jnp.float32) + other.astype(jnp.float32)).astype(value.dtype)


def add_other_core(keep, send, nodes, cores, scale):
    got = swap(send, cores, nodes * cores)
    slots, inner, rows, tile = keep.shape
    part = ((keep + got) * scale).astype(jnp.float16).reshape(cores, slots // cores, inner, rows, tile)
    return part[:, :, :, :rows // 2], part[:, :, :, rows // 2:]


def over_inner(value, nodes, cores):
    mask, index = 2 * cores, lax.axis_index("node") // 2
    while value.shape[2] > 1:
        value = halve(value, index % 2, 2, mask, nodes * cores)
        mask, index = mask * 2, index // 2
    return value


def over_low(value, nodes, cores):
    return halve(value, lax.axis_index("cores") % 2, 0, 1, nodes * cores)


def over_far(upper, lower, nodes, cores, scale):
    part = jnp.concatenate([upper, lower], axis=3)[:, :, 0]
    at = lax.axis_index("cores") // 2
    mine = pick(part, at, 0).astype(jnp.float32)
    for step in range(1, part.shape[0]):
        mine = mine + swap(pick(part, at ^ step, 0), 2 * step, nodes * cores).astype(jnp.float32)
    return mine * (0.5 / scale)


def pair_groups(partner_ref, pairs):
    count = jnp.int32(0)
    chosen = [jnp.int32(0)] * (pairs // 2)
    for p in range(pairs):
        is_rep = p < partner_ref[p]
        chosen = [jnp.where(is_rep & (count == g), p, old) for g, old in enumerate(chosen)]
        count = count + is_rep.astype(jnp.int32)
    return [(p, partner_ref[p]) for p in chosen]


def lower_kernel(partner_ref, amps_ref, *out_refs):
    for out_ref, both in zip(out_refs, pair_groups(partner_ref, amps_ref.shape[1])):
        for role, p in enumerate(both):
            out_ref[role] = amps_ref[:, p].astype(jnp.bfloat16)


def lower(partner, amplitudes):
    slots_here, pairs, rows, tile = amplitudes.shape
    vmem = pl.BlockSpec(memory_space=pltpu.VMEM)
    return pl.pallas_call(
        lower_kernel,
        out_shape=(jax.ShapeDtypeStruct((2, slots_here, rows, tile), jnp.bfloat16),) * (pairs // 2),
        in_specs=[pl.BlockSpec(memory_space=pltpu.SMEM), vmem],
        out_specs=(vmem,) * (pairs // 2),
        name="lower",
    )(partner, amplitudes)


def spread_far(part, cores, total):
    return [part] + [swap(part, 2 * step, total) for step in range(1, cores // 2)]


def spread_inner(parts, nodes, cores):
    total = nodes * cores
    first = jnp.stack([part[0] for part in parts])
    first = jnp.stack([first, swap(first, 1, total)])
    pieces = {0: jnp.stack([part[1] for part in parts])}
    bit = nodes // 2
    while bit > 1:
        pieces.update({other | bit: swap(piece, bit * cores, total) for other, piece in pieces.items()})
        bit //= 2
    return first, jnp.stack([pieces[2 * upper] for upper in range(nodes // 2)])


def spread_outer(first, second, nodes, cores):
    total = nodes * cores
    pieces = {0: first}
    bit = nodes // 2
    while bit > 1:
        pieces.update({other | bit: swap(piece, bit * cores, total) for other, piece in pieces.items()})
        bit //= 2
    return [pieces[2 * upper] for upper in range(1, nodes // 2)], swap(second, 1, total)


def spread_last(first, second, nodes, cores):
    total = nodes * cores
    return [swap(piece, cores, total) for piece in first], [swap(piece, cores, total) for piece in second]


def turn_blocks(mine, nodes, cores, scale):
    total = nodes * cores
    slots_here, rows, tile = mine.shape
    node_index = lax.axis_index("node")
    turned = (mine * scale).astype(jnp.float16).reshape(slots_here * rows, tile).T
    turned = turned.reshape(nodes, rows, slots_here * rows)
    pieces = [pick(turned, node_index, 0)]
    pieces += [swap(pick(turned, node_index ^ step, 0), step * cores, total) for step in range(1, nodes)]
    pieces = jnp.stack(pieces)
    block = jnp.stack([pick(pieces, node_index ^ n, 0) for n in range(nodes)])
    return block.reshape(nodes, rows, slots_here, rows).transpose(2, 1, 0, 3).reshape(slots_here, rows, tile)


def every_block(near, nodes, cores, scale):
    every = jnp.stack([near, swap(near, 1, nodes * cores)], axis=1)
    return every.reshape((cores,) + near.shape[1:]).astype(jnp.float32) * (1.0 / scale)


def update_kernel(side, owner_ref, partner_ref, pair_ref, energy_ref, column_ref, amps_ref, *refs):
    slots_here, pairs, rows, tile = amps_ref.shape
    groups = pairs // 2
    straight, crossed, out_ref, slot_of = refs[:groups], refs[groups:2 * groups], refs[-2], refs[-1]
    node_index = lax.axis_index("node")
    core_index = lax.axis_index("cores")

    def invert(s, carry):
        slot_of[owner_ref[s]] = s
        return carry

    lax.fori_loop(0, owner_ref.shape[0], invert, 0)
    for j in range(slots_here):
        mine = owner_ref[core_index * slots_here + j]
        row_tile, col_tile = mine // side, mine % side
        place = slot_of[col_tile * side + row_tile]
        apart, inside = (place // slots_here) ^ core_index, place % slots_here
        row_energy = energy_ref[pl.ds(pl.multiple_of(row_tile * tile + node_index * rows, 8), rows), :]
        col_energy = column_ref[pl.ds(col_tile, 1), :]
        for g, (rep, twin) in enumerate(pair_groups(partner_ref, pairs)):
            for p, value in ((rep, straight[g][j]), (twin, crossed[g][apart, inside])):
                denominator = (pair_ref[p] - row_energy) - col_energy
                out_ref[j, p] = amps_ref[j, p] + value / denominator


def update(owner_map, partner, pair_energy, virt_energy, amplitudes, straight, crossed):
    tile = amplitudes.shape[3]
    smem = pl.BlockSpec(memory_space=pltpu.SMEM)
    vmem = pl.BlockSpec(memory_space=pltpu.VMEM)
    return pl.pallas_call(
        functools.partial(update_kernel, math.isqrt(owner_map.shape[0])),
        out_shape=jax.ShapeDtypeStruct(amplitudes.shape, jnp.float32),
        in_specs=[smem] * 3 + [vmem] * (3 + len(straight) + len(crossed)),
        out_specs=vmem,
        scratch_shapes=[pltpu.SMEM(owner_map.shape, jnp.int32)],
        compiler_params=pltpu.CompilerParams(vmem_limit_bytes=32 * 1024 * 1024),
        name="update",
    )(
        owner_map, partner, pair_energy, virt_energy.reshape(-1, 1), virt_energy.reshape(-1, tile),
        amplitudes, *straight, *crossed,
    )


def body(nodes, cores, fitted, fit_mask, tasks, owner_map, partner, amplitudes, pair_energy, virt_energy):
    tile, aux = amplitudes.shape[3], fitted.shape[1] * nodes * cores
    largest = 2 * aux * min(tasks.shape[0], owner_map.shape[0]) * tile**2 * 0.09375**2 * 6.0
    scale = 2.0 ** -math.ceil(math.log2(largest / 65000.0))
    total = nodes * cores
    parts = lower(partner, amplitudes)
    groups = len(parts)
    barrier = lax.optimization_barrier

    amps = []
    for g in range(groups - 1):
        inner = spread_inner(spread_far(parts[g], cores, total), nodes, cores)
        outer = spread_outer(*inner, nodes, cores)
        first = [inner[0]] + outer[0]
        second = [inner[1], outer[1]]
        first_far, second_far = spread_last(first, second, nodes, cores)
        amps.append([piece for pair in zip(first, first_far) for piece in pair] + second + second_far)
    amps.append([lax.all_gather(parts[-1], AXES, axis=0, tiled=False)])
    sums = []
    for g in range(groups):
        sums.append(ladder_terms(fit_mask, tasks, owner_map, fitted, amps[g], nodes, cores))
    stages = [
        lambda v: add_other_core(*v, nodes, cores, scale),
        lambda v: barrier((over_inner(v[0], nodes, cores), over_low(v[1], nodes, cores))),
        lambda v: barrier((over_low(v[0], nodes, cores), over_inner(v[1], nodes, cores))),
        lambda v: over_far(*v, nodes, cores, scale),
        lambda v: turn_blocks(v, nodes, cores, scale),
        lambda v: jnp.stack(spread_far(v, cores, total)),
        lambda v: every_block(v, nodes, cores, scale),
    ]
    results = []
    for g in range(groups):
        results.append([sums[g]])
    for step in range(len(stages) + groups - 1):
        for g in reversed(range(groups)):
            stage = step - g
            if not 0 <= stage < len(stages):
                continue
            value = results[g][stage]
            if 0 < stage < 4 and g + 1 < groups and len(results[g + 1]) > 1:
                value = barrier((value, results[g + 1][-1]))[0]
            results[g].append(stages[stage](value))
    straight = [values[4] for values in results]
    crossed = [values[-1] for values in results]
    return update(owner_map, partner, pair_energy, virt_energy, amplitudes, straight, crossed)


def solution(mesh):
    placed = (P(None, AXES, None, None), P(), P(), P(), P(), P("cores", None, "node", None), P(), P())
    return jax.shard_map(
        functools.partial(body, mesh.shape["node"], mesh.shape["cores"]),
        mesh=mesh, in_specs=placed, out_specs=P("cores", None, "node", None), check_vma=False,
    )
```

```python
import functools
import math

import jax
import jax.numpy as jnp
from jax import lax
from jax.experimental import pallas as pl
from jax.experimental.pallas import tpu as pltpu
from jax.sharding import PartitionSpec as P

AXES = ("node", "cores")


def ladder_kernel(dims, mask_ref, tasks_ref, owner_ref, fitted_ref, *refs):
    nodes, cores, slots_here, rows, tile, aux, slots, side = dims
    amps_refs, refs = refs[:-11], refs[-11:]
    keep_ref, send_ref, left_buf, right_buf, half_buf, tile_buf, total, work, slot_of, load_sems, store_sems = refs
    task_count = tasks_ref.shape[0]
    node_index = lax.axis_index("node")
    core_index = lax.axis_index("cores")
    block = node_index * cores + core_index

    def invert(s, carry):
        slot_of[owner_ref[s]] = s
        return carry

    lax.fori_loop(0, slots, invert, 0)

    def indices(t):
        out_tile = tasks_ref[t, 0]
        in_tile = tasks_ref[t, 1]
        a, b = out_tile // side, out_tile % side
        c, d = in_tile // side, in_tile % side
        return a, b, a * side + c, b * side + d, in_tile

    def enlist(t, count):
        _, _, left, right, _ = indices(t)
        work[count] = t
        return count + mask_ref[left, block] * mask_ref[right, block]

    active = lax.fori_loop(0, task_count, enlist, jnp.int32(0))

    def start_loads(i, slot):
        _, _, left, right, in_tile = indices(work[i])
        pltpu.make_async_copy(fitted_ref.at[left], left_buf.at[slot], load_sems.at[slot, 0]).start()
        for q in range(aux):
            pltpu.make_async_copy(
                fitted_ref.at[right, q], right_buf.at[slot, :, pl.ds(q * tile, tile)], load_sems.at[slot, 1]
            ).start()
        place = slot_of[in_tile]
        inside = place % slots_here
        owner = place // slots_here
        apart = owner ^ core_index
        low, far = apart % 2, apart // 2

        def fetch(source, role, node):
            strip = pl.ds(pl.multiple_of(node * rows, rows), rows)
            pltpu.make_async_copy(source, tile_buf.at[slot, role, strip, :], load_sems.at[slot, 2]).start()

        if len(amps_refs) == 1:
            for node in range(nodes):
                fetch(amps_refs[0].at[node * cores + owner, :, inside], slice(None), node)
        else:
            first_refs, second_refs = amps_refs[:nodes], amps_refs[nodes:]
            for other in range(nodes):
                fetch(first_refs[other].at[low, far, inside], 0, node_index ^ other)
            for x in range(2):

                @pl.when(low == x)
                def _():
                    for other in range(nodes):
                        source = second_refs[(other % 2) * 2 + x].at[other // 2, far, inside]
                        fetch(source, 1, node_index ^ other)


    def wait_loads(slot):
        for k, buf in enumerate((left_buf, right_buf, tile_buf)):
            pltpu.make_async_copy(buf.at[slot], buf.at[slot], load_sems.at[slot, k]).wait()

    @pl.when(active > 0)
    def _():
        start_loads(0, 0)

    @pl.loop(0, slots)
    def _(s):
        total[s] = jnp.zeros(total.shape[1:], jnp.float32)

    def contract(first, second):
        return lax.dot_general(first, second, (((1,), (1,)), ((), ())), preferred_element_type=jnp.float32)

    @pl.loop(0, active)
    def _(i):
        slot = i % 2

        @pl.when(i + 1 < active)
        def _():
            start_loads(i + 1, 1 - slot)

        wait_loads(slot)
        a, b, _, _, _ = indices(work[i])
        straight = slot_of[a * side + b]
        crossed = slot_of[b * side + a]
        left_all = left_buf[slot].reshape(aux * tile, tile)
        for p in range(2):
            half = jnp.dot(left_all, tile_buf[slot, p], preferred_element_type=jnp.float32).astype(jnp.bfloat16)
            for q in range(aux):
                half_buf[p, :, q * tile:(q + 1) * tile] = half[q * tile:(q + 1) * tile]
        shape = total.shape[1:]
        total[straight] += contract(half_buf[0], right_buf[slot]).reshape(shape)
        total[crossed] += contract(right_buf[slot], half_buf[1]).reshape(shape)

    mine = node_index % 2
    stores = [
        pltpu.make_async_copy(total.at[:, :, mine], keep_ref, store_sems.at[0]),
        pltpu.make_async_copy(total.at[:, :, 1 - mine], send_ref, store_sems.at[1]),
    ]
    for copy in stores:
        copy.start()
    for copy in stores:
        copy.wait()


def ladder_terms(mask, tasks, owner_map, fitted, amps, nodes, cores):
    tile_pairs, aux, tile, _ = fitted.shape
    slots_here, rows = tile_pairs // cores, tile // nodes
    side = math.isqrt(tile_pairs)
    dims = (nodes, cores, slots_here, rows, tile, aux, tile_pairs, side)
    smem = pl.BlockSpec(memory_space=pltpu.SMEM)
    hbm = pl.BlockSpec(memory_space=pl.ANY)
    part = jax.ShapeDtypeStruct((tile_pairs, nodes // 2, rows, tile), jnp.float32)
    return pl.pallas_call(
        functools.partial(ladder_kernel, dims),
        out_shape=(part, part),
        in_specs=[smem, smem, smem] + [hbm] * (1 + len(amps)),
        out_specs=(hbm, hbm),
        scratch_shapes=[
            pltpu.VMEM((2, aux, tile, tile), jnp.bfloat16),
            pltpu.VMEM((2, tile, aux * tile), jnp.bfloat16),
            pltpu.VMEM((2, tile, aux * tile), jnp.bfloat16),
            pltpu.VMEM((2, 2, tile, tile), jnp.bfloat16),
            pltpu.VMEM((tile_pairs, nodes // 2, 2, rows, tile), jnp.float32),
            pltpu.SMEM((tasks.shape[0] + 1,), jnp.int32),
            pltpu.SMEM((tile_pairs,), jnp.int32),
            pltpu.SemaphoreType.DMA((2, 3)),
            pltpu.SemaphoreType.DMA((2,)),
        ],
        compiler_params=pltpu.CompilerParams(vmem_limit_bytes=58 * 1024 * 1024),
        cost_estimate=pl.CostEstimate(flops=20 * 10**9, bytes_accessed=30 * 2**20, transcendentals=0),
        name="ladder",
    )(mask, tasks, owner_map, fitted, *amps)


def swap(array, mask, total):
    return lax.ppermute(array, AXES, [(i, i ^ mask) for i in range(total)])


def pick(array, index, axis):
    return lax.dynamic_index_in_dim(array, index, axis, keepdims=False)


def halve(value, index, axis, mask, total):
    shape = value.shape
    split = value.reshape(shape[:axis] + (shape[axis] // 2, 2) + shape[axis + 1:])
    other = swap(pick(split, 1 - index, axis + 1), mask, total)
    own = pick(split, index, axis + 1)
    return (own.astype(jnp.float32) + other.astype(jnp.float32)).astype(value.dtype)


def add_other_core(keep, send, nodes, cores, scale):
    got = swap(send, cores, nodes * cores)
    slots, inner, rows, tile = keep.shape
    part = ((keep + got) * scale).astype(jnp.float16).reshape(cores, slots // cores, inner, rows, tile)
    return part[:, :, :, :rows // 2], part[:, :, :, rows // 2:]


def over_inner(value, nodes, cores):
    mask, index = 2 * cores, lax.axis_index("node") // 2
    while value.shape[2] > 1:
        value = halve(value, index % 2, 2, mask, nodes * cores)
        mask, index = mask * 2, index // 2
    return value


def over_low(value, nodes, cores):
    return halve(value, lax.axis_index("cores") % 2, 0, 1, nodes * cores)


def over_far(upper, lower, nodes, cores, scale):
    part = jnp.concatenate([upper, lower], axis=3)[:, :, 0]
    at = lax.axis_index("cores") // 2
    mine = pick(part, at, 0).astype(jnp.float32)
    for step in range(1, part.shape[0]):
        mine = mine + swap(pick(part, at ^ step, 0), 2 * step, nodes * cores).astype(jnp.float32)
    return mine * (0.5 / scale)


def pair_groups(partner_ref, pairs):
    count = jnp.int32(0)
    chosen = [jnp.int32(0)] * (pairs // 2)
    for p in range(pairs):
        is_rep = p < partner_ref[p]
        chosen = [jnp.where(is_rep & (count == g), p, old) for g, old in enumerate(chosen)]
        count = count + is_rep.astype(jnp.int32)
    return [(p, partner_ref[p]) for p in chosen]


def lower_kernel(partner_ref, amps_ref, *out_refs):
    for out_ref, both in zip(out_refs, pair_groups(partner_ref, amps_ref.shape[1])):
        for role, p in enumerate(both):
            out_ref[role] = amps_ref[:, p].astype(jnp.bfloat16)


def lower(partner, amplitudes):
    slots_here, pairs, rows, tile = amplitudes.shape
    vmem = pl.BlockSpec(memory_space=pltpu.VMEM)
    return pl.pallas_call(
        lower_kernel,
        out_shape=(jax.ShapeDtypeStruct((2, slots_here, rows, tile), jnp.bfloat16),) * (pairs // 2),
        in_specs=[pl.BlockSpec(memory_space=pltpu.SMEM), vmem],
        out_specs=(vmem,) * (pairs // 2),
        name="lower",
    )(partner, amplitudes)


def spread_far(part, cores, total):
    return [part] + [swap(part, 2 * step, total) for step in range(1, cores // 2)]


def spread_inner(parts, nodes, cores):
    total = nodes * cores
    first = jnp.stack([part[0] for part in parts])
    first = jnp.stack([first, swap(first, 1, total)])
    pieces = {0: jnp.stack([part[1] for part in parts])}
    bit = nodes // 2
    while bit > 1:
        pieces.update({other | bit: swap(piece, bit * cores, total) for other, piece in pieces.items()})
        bit //= 2
    return first, jnp.stack([pieces[2 * upper] for upper in range(nodes // 2)])


def spread_outer(first, second, nodes, cores):
    total = nodes * cores
    pieces = {0: first}
    bit = nodes // 2
    while bit > 1:
        pieces.update({other | bit: swap(piece, bit * cores, total) for other, piece in pieces.items()})
        bit //= 2
    return [pieces[2 * upper] for upper in range(1, nodes // 2)], swap(second, 1, total)


def spread_last(first, second, nodes, cores):
    total = nodes * cores
    return [swap(piece, cores, total) for piece in first], [swap(piece, cores, total) for piece in second]


def turn_blocks(mine, nodes, cores, scale):
    total = nodes * cores
    slots_here, rows, tile = mine.shape
    node_index = lax.axis_index("node")
    turned = (mine * scale).astype(jnp.float16).reshape(slots_here * rows, tile).T
    turned = turned.reshape(nodes, rows, slots_here * rows)
    pieces = [pick(turned, node_index, 0)]
    pieces += [swap(pick(turned, node_index ^ step, 0), step * cores, total) for step in range(1, nodes)]
    pieces = jnp.stack(pieces)
    block = jnp.stack([pick(pieces, node_index ^ n, 0) for n in range(nodes)])
    return block.reshape(nodes, rows, slots_here, rows).transpose(2, 1, 0, 3).reshape(slots_here, rows, tile)


def every_block(near, nodes, cores, scale):
    every = jnp.stack([near, swap(near, 1, nodes * cores)], axis=1)
    return every.reshape((cores,) + near.shape[1:]).astype(jnp.float32) * (1.0 / scale)


def update_kernel(side, owner_ref, partner_ref, pair_ref, energy_ref, column_ref, amps_ref, *refs):
    slots_here, pairs, rows, tile = amps_ref.shape
    groups = pairs // 2
    straight, crossed, out_ref, slot_of = refs[:groups], refs[groups:2 * groups], refs[-2], refs[-1]
    node_index = lax.axis_index("node")
    core_index = lax.axis_index("cores")

    def invert(s, carry):
        slot_of[owner_ref[s]] = s
        return carry

    lax.fori_loop(0, owner_ref.shape[0], invert, 0)
    for j in range(slots_here):
        mine = owner_ref[core_index * slots_here + j]
        row_tile, col_tile = mine // side, mine % side
        place = slot_of[col_tile * side + row_tile]
        apart, inside = (place // slots_here) ^ core_index, place % slots_here
        row_energy = energy_ref[pl.ds(pl.multiple_of(row_tile * tile + node_index * rows, 8), rows), :]
        col_energy = column_ref[pl.ds(col_tile, 1), :]
        for g, (rep, twin) in enumerate(pair_groups(partner_ref, pairs)):
            for p, value in ((rep, straight[g][j]), (twin, crossed[g][apart, inside])):
                denominator = (pair_ref[p] - row_energy) - col_energy
                out_ref[j, p] = amps_ref[j, p] + value / denominator


def update(owner_map, partner, pair_energy, virt_energy, amplitudes, straight, crossed):
    tile = amplitudes.shape[3]
    smem = pl.BlockSpec(memory_space=pltpu.SMEM)
    vmem = pl.BlockSpec(memory_space=pltpu.VMEM)
    return pl.pallas_call(
        functools.partial(update_kernel, math.isqrt(owner_map.shape[0])),
        out_shape=jax.ShapeDtypeStruct(amplitudes.shape, jnp.float32),
        in_specs=[smem] * 3 + [vmem] * (3 + len(straight) + len(crossed)),
        out_specs=vmem,
        scratch_shapes=[pltpu.SMEM(owner_map.shape, jnp.int32)],
        compiler_params=pltpu.CompilerParams(vmem_limit_bytes=32 * 1024 * 1024),
        name="update",
    )(
        owner_map, partner, pair_energy, virt_energy.reshape(-1, 1), virt_energy.reshape(-1, tile),
        amplitudes, *straight, *crossed,
    )


def body(nodes, cores, fitted, fit_mask, tasks, owner_map, partner, amplitudes, pair_energy, virt_energy):
    tile, aux = amplitudes.shape[3], fitted.shape[1] * nodes * cores
    largest = 2 * aux * min(tasks.shape[0], owner_map.shape[0]) * tile**2 * 0.09375**2 * 6.0
    scale = 2.0 ** -math.ceil(math.log2(largest / 65000.0))
    total = nodes * cores
    parts = lower(partner, amplitudes)
    groups = len(parts)
    barrier = lax.optimization_barrier

    amps = []
    for g in range(groups - 1):
        inner = spread_inner(spread_far(parts[g], cores, total), nodes, cores)
        outer = spread_outer(*inner, nodes, cores)
        first = [inner[0]] + outer[0]
        second = [inner[1], outer[1]]
        first_far, second_far = spread_last(first, second, nodes, cores)
        amps.append([piece for pair in zip(first, first_far) for piece in pair] + second + second_far)
    amps.append([lax.all_gather(parts[-1], AXES, axis=0, tiled=False)])
    sums = []
    for g in range(groups):
        sums.append(ladder_terms(fit_mask, tasks, owner_map, fitted, amps[g], nodes, cores))
    stages = [
        lambda v: add_other_core(*v, nodes, cores, scale),
        lambda v: barrier((over_inner(v[0], nodes, cores), over_low(v[1], nodes, cores))),
        lambda v: barrier((over_low(v[0], nodes, cores), over_inner(v[1], nodes, cores))),
        lambda v: over_far(*v, nodes, cores, scale),
        lambda v: turn_blocks(v, nodes, cores, scale),
        lambda v: jnp.stack(spread_far(v, cores, total)),
        lambda v: every_block(v, nodes, cores, scale),
    ]
    results = []
    for g in range(groups):
        results.append([sums[g]])
    for step in range(len(stages) + groups - 1):
        for g in reversed(range(groups)):
            stage = step - g
            if not 0 <= stage < len(stages):
                continue
            value = results[g][stage]
            if 0 < stage < 4 and g + 1 < groups and len(results[g + 1]) > 1:
                value = barrier((value, results[g + 1][-1]))[0]
            results[g].append(stages[stage](value))
    straight = [values[4] for values in results]
    crossed = [values[-1] for values in results]
    return update(owner_map, partner, pair_energy, virt_energy, amplitudes, straight, crossed)


def solution(mesh):
    placed = (P(None, AXES, None, None), P(), P(), P(), P(), P("cores", None, "node", None), P(), P())
    return jax.shard_map(
        functools.partial(body, mesh.shape["node"], mesh.shape["cores"]),
        mesh=mesh, in_specs=placed, out_specs=P("cores", None, "node", None), check_vma=False,
    )
```
